256 devices in a mesh: row: 32 (over y, z), col: 8 (over x, core).
Axes of the slice: x: 4, y: 4, z: 8, core: 2. Of those that a mesh axis runs over, the one named last changes fastest.
Arguments:
- ancestor_inverse: float32 [12288, 12288], P('row', 'col'), may hold values from -5 to 320, as said below
- panel_one: float32 [12288, 256], P(('row', 'col')), may hold values from -0.015625 to 0.015625
- struct_one: int32 [10752], replicated, may hold values from 0 to 12287, as said below
- lower_one: float32 [256, 256], replicated, may hold values from -1 to 2, as said below
- panel_two: float32 [12288, 256], P(('row', 'col')), may hold values from -0.015625 to 0.015625
- struct_two: int32 [9216], replicated, may hold values from 0 to 12287, as said below
- panel_above: float32 [256, 256], replicated, may hold values from -0.375 to 0.375
- lower_two: float32 [256, 256], replicated, may hold values from -1 to 2, as said below
- tile_owner: int32 [1536, 1], P(('col', 'row')), may hold values from 0 to 7; in each aligned block of 6 rows (0 to 5, 6 to 11, ...) at most 2 rows name the same one
Outputs:
- inverse_one: float32 [12288, 256], P(('col', 'row'))
- diag_one: float32 [256, 256], replicated
- cross_two: float32 [256, 256], replicated
- diag_two: float32 [256, 256], replicated
- delivered: float32 [4096, 8, 256], P(('row', 'col'))
The draws below stay inside these ranges and needn't reach their ends.
Inputs may be any that keep to these rules, and one draw needn't show every extreme that they name: ancestor_inverse is exactly symmetric and positive definite. `struct_one`: 10752 distinct row numbers of the ancestor block. `struct_two`: 9216 distinct entries of struct_one. `lower_one`: lower triangular with a positive diagonal. `lower_two`: lower triangular with a positive diagonal. `tile_owner`: within each aligned block of 6 entries (the tiles of one device) no value appears more than 2 times; in some block a value appears exactly 2 times.
All inputs are finite; a program needn't handle non-finite values.
Results may differ from the reference program's by a relative error of at most 0.00007.
Values sent between devices are 32-bit elements; how exact they have to be, the bound alone decides.
No kernel may reach another device: no remote copies, remote signals or barrier semaphores. Data moves between devices by JAX's collectives and lax.ppermute only.
A program may use at most 64 MiB of HBM per device.

```python
import math
import jax
import jax.numpy as jnp
import numpy as np
from jax import lax

ANC = 12288
SUPER = 256
R_ONE = 10752
R_TWO = 9216
TILES_DEV = 6
CAP = 2
N_ROW = 32
N_COL = 8
DEVICES = 256


def draw_ancestor_inverse(key, part):
    first, second = jax.random.split(jax.random.fold_in(key, 11), 2)
    entries = jax.random.truncated_normal(first, -6.0, 6.0, (ANC, ANC), jnp.float32)
    upper_part = jnp.triu(entries, 1)
    diagonal_values = jax.random.uniform(second, (ANC,), jnp.float32, 2.5, 5.0)
    matrix = 16.0 * (jnp.diag(diagonal_values) + 0.8 / (2.0 * ANC) ** 0.5 * (upper_part + upper_part.T))
    return matrix


def structure_lists(key):
    first, second, third = jax.random.split(jax.random.fold_in(key, 23), 3)
    positions = jnp.arange(ANC, dtype=jnp.int32)
    region = positions // (ANC // 16)
    base_score = jax.random.randint(first, (ANC,), 0, 2 ** 14, dtype=jnp.int32)
    region_lift = jax.random.randint(second, (16,), 0, 2 ** 15, dtype=jnp.int32)
    scores = (base_score + region_lift[region]) * ANC + positions
    chosen = lax.top_k(scores, R_ONE)[1].astype(jnp.int32)
    shuffle = jax.random.permutation(third, R_ONE)
    return (chosen, chosen[shuffle[:R_TWO]].astype(jnp.int32))


def draw_struct_one(key, part):
    return structure_lists(key)[0]


def draw_struct_two(key, part):
    return structure_lists(key)[1]


def lower_factor(key):
    first, second = jax.random.split(key, 2)
    lower_part = jnp.tril(jax.random.truncated_normal(first, -4.0, 4.0, (SUPER, SUPER), jnp.float32) * (0.5 / SUPER ** 0.5), -1)
    diagonal_values = jnp.exp(jax.random.uniform(second, (SUPER,), jnp.float32, math.log(0.5), math.log(2.0)))
    return lower_part + jnp.diag(diagonal_values)


def draw_lower_one(key, part):
    return lower_factor(jax.random.fold_in(key, 31))


def draw_lower_two(key, part):
    return lower_factor(jax.random.fold_in(key, 37))


def level_of(own_key, dims, shards, low, high):
    def one(axis_at, shards_of):
        heights = jax.random.uniform(jax.random.fold_in(jax.random.fold_in(own_key, 6), axis_at), (shards_of,), jnp.float32, low / len(shards), high / len(shards))
        return jnp.repeat(jnp.exp(heights), dims[axis_at] // shards_of).reshape((-1,) + (1,) * (len(dims) - axis_at - 1))

    loudness = one(*shards[0])
    for cut in shards[1:]:
        loudness = loudness * one(*cut)
    return loudness


def assign_block(key, own, number, rows, amount, top, most, skew):
    ranking = jax.random.permutation(key, amount)
    heavy_load, common = shares(amount, rows * top, most, skew, True), shares(amount, rows * top, most, skew, False)
    places = jnp.arange(amount)

    def named(tallies, turn):
        used = int((tallies > 0).sum())
        fixed = max(1, used // 4)
        shifted = fixed + (places - fixed + turn * (used - fixed)) % max(1, amount - fixed)
        return jnp.zeros((amount,), jnp.int32).at[ranking[jnp.where(places < fixed, places, shifted)]].set(jnp.asarray(tallies, jnp.int32))

    tallies = jnp.where(number % 4 == 0, named(heavy_load, number // 4), named(common, number - number // 4 - 1))
    mixed = jax.random.permutation(jax.random.fold_in(own, 3), amount)
    giver, receiver = mixed[0:amount // 2 * 2:2], mixed[1:amount // 2 * 2:2]
    slack = jnp.minimum(tallies[giver] - 1, most - tallies[receiver]) // 2
    slack = jnp.where((giver == ranking[0]) | (receiver == ranking[0]) | (tallies[receiver] == 0), 0, jnp.maximum(slack, 0))
    shifted = jax.random.randint(jax.random.fold_in(own, 4), (amount // 2,), 0, 1 << 20) % (slack + 1)
    tallies = tallies.at[giver].add(-shifted).at[receiver].add(shifted)
    members = jnp.searchsorted(jnp.cumsum(tallies), jnp.arange(rows * top), side="right").astype(jnp.int32)
    grid = members.reshape(top, rows).T
    grid = grid[jax.random.permutation(jax.random.fold_in(own, 1), rows)]
    turn = jax.random.randint(jax.random.fold_in(own, 2), (rows, 1), 0, top)
    return jnp.take_along_axis(grid, (jnp.arange(top)[None, :] + turn) % top, axis=1)


def shares(count, total, bound, skew, full):
    weights = [(1 << 20) // math.isqrt(grade ** skew) + 1 for grade in range(1, count + 1)]
    largest = bound if full else min(bound, max(-(-total // count), total * weights[0] // sum(weights)))
    least = 1 if total - largest >= count - 1 else 0
    counts, rest = [largest] + [least] * (count - 1), total - largest - least * (count - 1)
    while rest > 0:
        free = [i for i in range(1, count) if counts[i] < largest] or [i for i in range(1, count) if counts[i] < bound]
        whole, left = sum([weights[i] for i in free]), rest
        for i in free:
            extra = min(bound - counts[i], max(1, left * weights[i] // whole), rest)
            counts[i] = counts[i] + extra
            rest = rest - extra
    return np.array(counts)


def normal_values(own_key, extent, deviation, limit, cuts=(), held_as=jnp.bfloat16):
    level = level_of(own_key, extent, cuts, -0.22, 0.18) if cuts else 1.0
    drawn = jax.random.normal(own_key, extent, jnp.float32) * deviation * level
    return jnp.minimum(jnp.maximum(drawn, -limit), limit).astype(held_as)


def setup_inputs(seed: int = 0) -> dict:
    splits = jax.random.split(jax.random.key(seed), 10)
    ancestor_inverse = draw_ancestor_inverse(jax.random.fold_in(splits[9], 71), 0)
    panel_one = normal_values(splits[1], (ANC, SUPER), (15 * R_ONE) ** -0.5, 0.015625, ((0, 256),), jnp.float32)
    struct_one = draw_struct_one(jax.random.fold_in(splits[9], 71), 0)
    lower_one = draw_lower_one(jax.random.fold_in(splits[9], 71), 0)
    panel_two = normal_values(splits[4], (ANC, SUPER), (15 * R_TWO) ** -0.5, 0.015625, ((0, 256),), jnp.float32)
    struct_two = draw_struct_two(jax.random.fold_in(splits[9], 71), 0)
    panel_above = normal_values(splits[6], (SUPER, SUPER), SUPER ** -0.5, 0.375, (), jnp.float32)
    lower_two = draw_lower_two(jax.random.fold_in(splits[9], 71), 0)
    tile_owner_keys = jax.random.split(jax.random.fold_in(splits[8], 1), (DEVICES * TILES_DEV) // TILES_DEV)
    tile_owner_turns = jax.random.permutation(jax.random.fold_in(splits[8], 3), (DEVICES * TILES_DEV) // TILES_DEV)
    tile_owner = jax.vmap(lambda own, number: assign_block(jax.random.fold_in(splits[8], 2), own, number, TILES_DEV, N_COL, 1, CAP, 2))(tile_owner_keys, tile_owner_turns).reshape((DEVICES * TILES_DEV, 1))
    return dict(ancestor_inverse=ancestor_inverse, panel_one=panel_one, struct_one=struct_one, lower_one=lower_one, panel_two=panel_two, struct_two=struct_two, panel_above=panel_above, lower_two=lower_two, tile_owner=tile_owner)


def matmul(left, right):
    return jnp.dot(left, right, precision=lax.Precision.HIGHEST, preferred_element_type=jnp.float32)


def deliver(values, tile_owner):
    tile_rows = ANC // (N_ROW * N_COL * TILES_DEV)
    tile_count = ANC // tile_rows
    all_tiles = values.reshape(tile_count, tile_rows, SUPER)
    owner_col = tile_owner[:, 0].astype(jnp.int32)
    onehot = (owner_col[:, None] == jnp.arange(N_COL, dtype=jnp.int32)[None, :]).astype(jnp.int32)
    grouped = onehot.reshape(tile_count // TILES_DEV, TILES_DEV, N_COL)
    earlier = jnp.cumsum(grouped, axis=1) - grouped
    tile_rank = jnp.sum(earlier * grouped, axis=2).reshape(tile_count)
    tile_group = jnp.arange(tile_count, dtype=jnp.int32) // TILES_DEV
    source_row = tile_group % N_ROW
    source_col = tile_group // N_ROW
    target = ((source_row * N_COL + owner_col) * N_COL + source_col) * CAP + tile_rank
    empty_slots = jnp.zeros((N_ROW * N_COL * N_COL * CAP, tile_rows, SUPER), jnp.float32)
    return empty_slots.at[target.astype(jnp.int32)].set(all_tiles)


def reference(ancestor_inverse, panel_one, struct_one, lower_one, panel_two, struct_two, panel_above, lower_two, tile_owner):
    mask_one = jnp.zeros((ANC,), jnp.float32).at[struct_one].set(1.0)
    mask_two = jnp.zeros((ANC,), jnp.float32).at[struct_two].set(1.0)
    masked_one = panel_one * mask_one[:, None]
    masked_two = panel_two * mask_two[:, None]
    inverse_one = -matmul(ancestor_inverse, masked_one) * mask_one[:, None]
    diag_one = matmul(lower_one.T, lower_one) - matmul(masked_one.T, inverse_one)
    inverse_two = -(matmul(ancestor_inverse, masked_two) + matmul(inverse_one, panel_above)) * mask_two[:, None]
    cross_two = -(matmul(inverse_one.T, masked_two) + matmul(diag_one, panel_above))
    diag_two = matmul(lower_two.T, lower_two) - matmul(masked_two.T, inverse_two) - matmul(panel_above.T, cross_two)
    delivered = deliver(inverse_two, tile_owner)
    return inverse_one, diag_one, cross_two, diag_two, delivered
```

```python
import jax
import jax.numpy as jnp
from jax import lax
from jax.sharding import Mesh
from jax.sharding import PartitionSpec as P

CAP = 2
COL = ("col_0", "col_1")
ROW = ("row_0", "row_1")
ROW_COL = ROW + COL
COL_ROW = COL + ROW
N_ROW = 32
N_COL = 8
N_Y, N_Z = 4, 8


def row_mask(listed, start, count):
    rows = start + jnp.arange(count, dtype=jnp.int32)
    hit = listed[None, :] == rows[:, None]
    return jnp.max(jnp.where(hit, 1.0, 0.0), axis=1, keepdims=True)


def dot(left, right, dims=((1,), (0,)), precision=lax.Precision.HIGHEST):
    return lax.dot_general(
        left, right, (dims, ((), ())), precision=precision, preferred_element_type=jnp.float32
    )


def sum_at_owner(value, axis):
    count = lax.axis_size(axis)
    parts = value.reshape(count, value.shape[0] // count, *value.shape[1:])
    return jnp.sum(lax.all_to_all(parts, axis, 0, 0, tiled=True), axis=0)


def copies_of(value, axis):
    copies = jnp.broadcast_to(value[None], (lax.axis_size(axis), *value.shape))
    return lax.all_to_all(copies, axis, 0, 0, tiled=True)


def total(value):
    own = sum_at_owner(sum_at_owner(value, COL), ROW)
    over_row = copies_of(own, ROW).reshape(-1, value.shape[1])
    return copies_of(over_row, COL).reshape(value.shape)


def gather_moves():
    pairs = []
    for block in range(N_ROW * N_COL):
        column, place = divmod(block, N_ROW)
        z, y = divmod(place, N_Y)
        pairs.append((block, (y * N_Z + z) * N_COL + column))
    return pairs


def result_moves():
    pairs = []
    for block in range(N_ROW * N_COL):
        column, row = divmod(block, N_ROW)
        pairs.append((block, row * N_COL + column))
    return pairs


def deliver(values, tile_owner):
    tile_count = tile_owner.shape[0]
    tile_rows = values.shape[0] // tile_count
    all_tiles = values.reshape(tile_count, tile_rows, values.shape[1])
    owner = tile_owner[:, 0]
    order = jnp.arange(tile_count)
    same = (owner[:, None] == owner[None, :]) & (order[None, :] < order[:, None])
    rank = jnp.sum(same.astype(jnp.int32), axis=1)
    select = (
        (owner[None, None, :] == jnp.arange(N_COL)[:, None, None])
        & (rank[None, None, :] == jnp.arange(CAP)[None, :, None])
    ).astype(jnp.float32)
    outgoing = jnp.einsum("cks,srb->ckrb", select, all_tiles, precision=lax.Precision.HIGHEST)
    incoming = lax.all_to_all(outgoing, COL, split_axis=0, concat_axis=0, tiled=True)
    return incoming.reshape(N_COL * CAP, tile_rows, values.shape[1])


def local(
    ancestor_inverse,
    panel_one,
    struct_one,
    lower_one,
    panel_two,
    struct_two,
    panel_above,
    lower_two,
    tile_owner,
):
    row_index = lax.axis_index(ROW)
    col_index = lax.axis_index(COL)
    local_rows, width = panel_one.shape
    start = (row_index * N_COL + col_index) * local_rows
    mask_one = row_mask(struct_one, start, local_rows)
    mask_two = row_mask(struct_two, start, local_rows)
    panels = jnp.concatenate([panel_one * mask_one, panel_two * mask_two], axis=1)
    placed = lax.ppermute(panels, ROW_COL, gather_moves())
    column_panels = lax.all_gather(placed, "row_0", axis=0, tiled=True)
    column_panels = lax.all_gather(column_panels, "row_1", axis=0, tiled=True)
    row_panels = lax.all_gather(panels, COL, axis=0, tiled=True)
    product = dot(ancestor_inverse, column_panels, precision=lax.Precision.HIGH)
    from_one = dot(row_panels[:, :width], product, ((0,), (0,)), lax.Precision.HIGH)
    from_two = dot(row_panels[:, width:], product[:, width:], ((0,), (0,)), lax.Precision.HIGH)
    partial = jnp.concatenate([from_one[:, :width], from_one[:, width:], from_two], axis=0)
    grams = total(partial)
    w_one, w_cross, w_two = grams[:width], grams[width : 2 * width], grams[2 * width :]
    diag_one = dot(lower_one, lower_one, ((0,), (0,))) + w_one
    cross_two = w_cross - dot(diag_one, panel_above)
    diag_two = (
        dot(lower_two, lower_two, ((0,), (0,)))
        + w_two
        - dot(w_cross, panel_above, ((0,), (0,)))
        - dot(panel_above, cross_two, ((0,), (0,)))
    )
    rows = sum_at_owner(product, COL)
    inverse_one = -rows[:, :width] * mask_one
    inverse_two = -(rows[:, width:] + dot(inverse_one, panel_above)) * mask_two
    inverses = lax.ppermute(
        jnp.concatenate([inverse_one, inverse_two], axis=1), ROW_COL, result_moves()
    )
    inverse_one, inverse_two = inverses[:, :width], inverses[:, width:]
    delivered = deliver(inverse_two, tile_owner)
    return (inverse_one, diag_one, cross_two, diag_two, delivered)


def solution(mesh):
    finer = Mesh(mesh.devices.reshape(4, 8, 4, 2), ("row_0", "row_1", "col_0", "col_1"))
    return jax.shard_map(
        local,
        mesh=finer,
        in_specs=(
            P(ROW, COL),
            P(ROW_COL, None),
            P(),
            P(),
            P(ROW_COL, None),
            P(),
            P(),
            P(),
            P(COL_ROW, None),
        ),
        out_specs=(P(COL_ROW, None), P(), P(), P(), P(ROW_COL, None, None)),
        check_vma=False,
    )
```

```python
import jax
import jax.numpy as jnp
from jax import lax
from jax.experimental import pallas as pl
from jax.experimental.pallas import tpu as pltpu
from jax.sharding import Mesh
from jax.sharding import PartitionSpec as P

CAP = 2
COL = ("col_0", "col_1")
ROW = ("row_0", "row_1")
ROW_COL = ROW + COL
COL_ROW = COL + ROW
PLANE = ("row_0", "col_0")
N_Y, N_Z, N_X, N_K = 4, 8, 4, 2
N_ROW, N_COL = N_Y * N_Z, N_X * N_K
ROWS = 48
WIDTH = 256


def device(y, z, x, k):
    return ((y * N_Z + z) * N_X + x) * N_K + k


def moves(place):
    return [
        (device(y, z, x, k), device(*place(y, z, x, k)))
        for y in range(N_Y)
        for z in range(N_Z)
        for x in range(N_X)
        for k in range(N_K)
    ]


def to_column(step):
    return moves(lambda y, z, x, k: ((x + step) % N_Y, 2 * (z % 4) + k, y, z // 4))


def result_place(y, z, x, k):
    column, row = divmod((y * N_Z + z) * N_COL + x * N_K + k, N_ROW)
    return (row // N_Z, row % N_Z, column // N_K, column % N_K)


def along_y(step):
    return moves(lambda y, z, x, k: ((y + step) % N_Y, z, x, k))


def other_core():
    return moves(lambda y, z, x, k: (y, z, x, 1 - k))


def row_mask(listed, start, count):
    rows = start + jnp.arange(count, dtype=jnp.int32)
    hit = listed[None, :] == rows[:, None]
    return jnp.max(jnp.where(hit, 1.0, 0.0), axis=1, keepdims=True)


def dot(left, right, dims=((1,), (0,)), precision=lax.Precision.HIGHEST):
    return lax.dot_general(
        left, right, (dims, ((), ())), precision=precision, preferred_element_type=jnp.float32
    )


def split(value):
    high = value.astype(jnp.bfloat16)
    return high, (value - high.astype(jnp.float32)).astype(jnp.bfloat16)


def three_pass(left, right, dims):
    (a, b), (c, d) = left, right

    def one(p, q):
        return lax.dot_general(p, q, (dims, ((), ())), preferred_element_type=jnp.float32)

    return one(a, c) + (one(a, d) + one(b, c))


def product_kernel(
    place, a_ref, g0_ref, g1_ref, g2_ref, g3_ref, own_ref, other_ref,
    w_keep, w_send, y_keep, y_send, xh, xl, rh, rl, w_all, y_all,
):
    y, k = place[0], place[1]
    for step, g_ref in enumerate((g0_ref, g1_ref, g2_ref, g3_ref)):
        x = lax.rem(y + step, N_X)
        for q in range(4):
            high, low = split(g_ref[pl.ds(q * 96, 96), :])
            at = pl.multiple_of(q * 384 + x * 96, 32)
            xh[pl.ds(at, 96), :] = high
            xl[pl.ds(at, 96), :] = low
    for x in range(N_X):
        for ref, core in ((own_ref, k), (other_ref, 1 - k)):
            high, low = split(ref[x])
            at = pl.multiple_of((x * N_K + core) * ROWS, 16)
            rh[pl.ds(at, ROWS), :] = high
            rl[pl.ds(at, ROWS), :] = low
    product = three_pass(split(a_ref[...]), (xh[...], xl[...]), ((1,), (0,)))
    for block in range(N_COL):
        y_all[block] = product[block * ROWS : (block + 1) * ROWS]
    high, low = split(product)
    rows_dims = ((0,), (0,))
    one = (rh[:, :WIDTH], rl[:, :WIDTH])
    two = (rh[:, WIDTH:], rl[:, WIDTH:])
    from_one = three_pass(one, (high, low), rows_dims)
    w_all[0:WIDTH, :] = from_one[:, :WIDTH]
    w_all[WIDTH : 2 * WIDTH, :] = from_one[:, WIDTH:]
    w_all[2 * WIDTH :, :] = three_pass(two, (high[:, WIDTH:], low[:, WIDTH:]), rows_dims)
    half = 3 * WIDTH // 2
    w_keep[...] = w_all[pl.ds(pl.multiple_of(k * half, 128), half), :]
    w_send[...] = w_all[pl.ds(pl.multiple_of((1 - k) * half, 128), half), :]
    for x in range(N_X):
        y_keep[x] = y_all[x * N_K + k]
        y_send[x] = y_all[x * N_K + 1 - k]


def product_and_grams(place, ancestor, gathered, own, other):
    f32, bf16 = jnp.float32, jnp.bfloat16
    half = 3 * WIDTH // 2
    wide = 2 * WIDTH
    vmem = pl.BlockSpec(memory_space=pltpu.VMEM)
    return pl.pallas_call(
        product_kernel,
        in_specs=[pl.BlockSpec(memory_space=pltpu.SMEM)] + [vmem] * 7,
        out_specs=[vmem] * 4,
        out_shape=[
            jax.ShapeDtypeStruct((half, WIDTH), f32),
            jax.ShapeDtypeStruct((half, WIDTH), f32),
            jax.ShapeDtypeStruct((N_X, ROWS, wide), f32),
            jax.ShapeDtypeStruct((N_X, ROWS, wide), f32),
        ],
        scratch_shapes=[
            pltpu.VMEM((1536, wide), bf16),
            pltpu.VMEM((1536, wide), bf16),
            pltpu.VMEM((384, wide), bf16),
            pltpu.VMEM((384, wide), bf16),
            pltpu.VMEM((3 * WIDTH, WIDTH), f32),
            pltpu.VMEM((N_COL, ROWS, wide), f32),
        ],
        compiler_params=pltpu.CompilerParams(vmem_limit_bytes=48 * 1024 * 1024),
        name="product_and_grams",
    )(place, ancestor, *gathered, own, other)


def at_owner(value, axis):
    count = lax.axis_size(axis)
    parts = value.reshape(count, value.shape[0] // count, *value.shape[1:])
    return lax.all_to_all(parts, axis, 0, 0, tiled=True)


def copies_of(value, axis):
    copies = jnp.broadcast_to(value[None], (lax.axis_size(axis), *value.shape))
    return lax.all_to_all(copies, axis, 0, 0, tiled=True)


def selection(tile_owner):
    tile_count = tile_owner.shape[0]
    owner = tile_owner[:, 0]
    order = jnp.arange(tile_count)
    same = (owner[:, None] == owner[None, :]) & (order[None, :] < order[:, None])
    rank = jnp.sum(same.astype(jnp.int32), axis=1)
    return (
        (owner[None, None, :] == jnp.arange(N_COL)[:, None, None])
        & (rank[None, None, :] == jnp.arange(CAP)[None, :, None])
    ).astype(jnp.float32)


def deliver(values, select):
    tile_count = select.shape[2]
    tile_rows = values.shape[0] // tile_count
    all_tiles = values.reshape(tile_count, tile_rows, values.shape[1])
    outgoing = jnp.einsum("cks,srb->ckrb", select, all_tiles, precision=lax.Precision.HIGHEST)
    incoming = lax.all_to_all(outgoing, COL, split_axis=0, concat_axis=0, tiled=True)
    return incoming.reshape(N_COL * CAP, tile_rows, values.shape[1])


def local(
    ancestor_inverse,
    panel_one,
    struct_one,
    lower_one,
    panel_two,
    struct_two,
    panel_above,
    lower_two,
    tile_owner,
):
    start = (lax.axis_index(ROW) * N_COL + lax.axis_index(COL)) * ROWS
    mask_one = row_mask(struct_one, start, ROWS)
    mask_two = row_mask(struct_two, start, ROWS)
    panels = jnp.concatenate([panel_one * mask_one, panel_two * mask_two], axis=1)
    block = lax.ppermute(panels, ROW_COL, to_column(0))
    far_block = lax.ppermute(panels, ROW_COL, to_column(2))
    own_core = lax.all_gather(panels, "col_0", axis=0)
    next_core = lax.ppermute(own_core, ROW_COL, other_core())
    gathered = lax.all_gather(block, "row_1", axis=0, tiled=True)
    above = lax.ppermute(gathered, ROW_COL, along_y(-1))
    below = lax.ppermute(gathered, ROW_COL, along_y(1))
    far_block, _ = lax.optimization_barrier((far_block, gathered))
    far = lax.all_gather(far_block, "row_1", axis=0, tiled=True)
    place = jnp.stack([lax.axis_index("row_0"), lax.axis_index("col_1")]).astype(jnp.int32)
    w_keep, w_send, y_keep, y_send = product_and_grams(
        place, ancestor_inverse, (gathered, above, far, below), own_core, next_core
    )
    w_own = w_keep + lax.ppermute(w_send, ROW_COL, other_core())
    y_own = y_keep + lax.ppermute(y_send, ROW_COL, other_core())
    w_part = jnp.sum(at_owner(w_own, PLANE), axis=0)
    w_part = jnp.sum(copies_of(w_part, "row_1"), axis=0)
    w_half = copies_of(w_part, PLANE).reshape(w_own.shape)
    w_other = lax.ppermute(w_half, ROW_COL, other_core())
    first = lax.axis_index("col_1") == 0
    grams = jnp.concatenate(
        [jnp.where(first, w_half, w_other), jnp.where(first, w_other, w_half)], axis=0
    )
    w_one, w_cross, w_two = grams[:WIDTH], grams[WIDTH : 2 * WIDTH], grams[2 * WIDTH :]
    diag_one = dot(lower_one, lower_one, ((0,), (0,))) + w_one
    cross_two = w_cross - dot(diag_one, panel_above)
    diag_two = (
        dot(lower_two, lower_two, ((0,), (0,)))
        + w_two
        - dot(w_cross, panel_above, ((0,), (0,)))
        - dot(panel_above, cross_two, ((0,), (0,)))
    )
    rows = jnp.sum(lax.all_to_all(y_own, "col_0", 0, 0, tiled=True), axis=0)
    inverse_one = -rows[:, :WIDTH] * mask_one
    inverse_two = -(rows[:, WIDTH:] + dot(inverse_one, panel_above)) * mask_two
    inverses = lax.ppermute(
        jnp.concatenate([inverse_one, inverse_two], axis=1), ROW_COL, moves(result_place)
    )
    inverse_one, inverse_two = inverses[:, :WIDTH], inverses[:, WIDTH:]
    delivered = deliver(inverse_two, selection(tile_owner))
    return (inverse_one, diag_one, cross_two, diag_two, delivered)


def solution(mesh):
    finer = Mesh(mesh.devices.reshape(4, 8, 4, 2), ("row_0", "row_1", "col_0", "col_1"))
    return jax.shard_map(
        local,
        mesh=finer,
        in_specs=(
            P(ROW, COL),
            P(ROW_COL, None),
            P(),
            P(),
            P(ROW_COL, None),
            P(),
            P(),
            P(),
            P(COL_ROW, None),
        ),
        out_specs=(P(COL_ROW, None), P(), P(), P(), P(ROW_COL, None, None)),
        check_vma=False,
    )
```

```python
import jax
import jax.numpy as jnp
from jax import lax
from jax.experimental import pallas as pl
from jax.experimental.pallas import tpu as pltpu
from jax.sharding import Mesh
from jax.sharding import PartitionSpec as P

CAP = 2
COL = ("col_0", "col_1")
ROW = ("row_0", "row_1")
ROW_COL = ROW + COL
COL_ROW = COL + ROW
PLANE = ("row_0", "col_0")
N_Y, N_Z, N_X, N_K = 4, 8, 4, 2
N_ROW, N_COL = N_Y * N_Z, N_X * N_K
ROWS = 48
WIDTH = 256


def device(y, z, x, k):
    return ((y * N_Z + z) * N_X + x) * N_K + k


def moves(place):
    return [
        (device(y, z, x, k), device(*place(y, z, x, k)))
        for y in range(N_Y)
        for z in range(N_Z)
        for x in range(N_X)
        for k in range(N_K)
    ]


def to_column(step):
    return moves(lambda y, z, x, k: ((x + step) % N_Y, 2 * (z % 4) + k, y, z // 4))


def result_place(y, z, x, k):
    column, row = divmod((y * N_Z + z) * N_COL + x * N_K + k, N_ROW)
    return (row // N_Z, row % N_Z, column // N_K, column % N_K)


def along_y(step):
    return moves(lambda y, z, x, k: ((y + step) % N_Y, z, x, k))


def along_x(step):
    return moves(lambda y, z, x, k: (y, z, (x + step) % N_X, k))


def other_core():
    return moves(lambda y, z, x, k: (y, z, x, 1 - k))


def row_mask(listed, start, count):
    rows = start + jnp.arange(count, dtype=jnp.int32)
    hit = listed[None, :] == rows[:, None]
    return jnp.max(jnp.where(hit, 1.0, 0.0), axis=1, keepdims=True)


def dot(left, right, dims=((1,), (0,)), precision=lax.Precision.HIGHEST):
    return lax.dot_general(
        left, right, (dims, ((), ())), precision=precision, preferred_element_type=jnp.float32
    )


def split(value):
    high = value.astype(jnp.bfloat16)
    return high, (value - high.astype(jnp.float32)).astype(jnp.bfloat16)


def three_pass(left, right, dims):
    (a, b), (c, d) = left, right

    def one(p, q):
        return lax.dot_general(p, q, (dims, ((), ())), preferred_element_type=jnp.float32)

    return one(a, c) + (one(a, d) + one(b, c))


def product_kernel(
    place, a_ref, g0_ref, g1_ref, g2_ref, g3_ref, own_ref, other_ref,
    w_keep, w_send, y_keep, y_send, xh, xl, rh, rl, w_all, y_all,
):
    y, column, k = place[0], place[1], place[2]
    for step, g_ref in enumerate((g0_ref, g1_ref, g2_ref, g3_ref)):
        x = lax.rem(y + step, N_X)
        for q in range(4):
            high, low = split(g_ref[pl.ds(q * 96, 96), :])
            at = pl.multiple_of(q * 384 + x * 96, 32)
            xh[pl.ds(at, 96), :] = high
            xl[pl.ds(at, 96), :] = low
    for x in range(N_X):
        for ref, core in ((own_ref, k), (other_ref, 1 - k)):
            high, low = split(ref[x])
            at = pl.multiple_of((x * N_K + core) * ROWS, 16)
            rh[pl.ds(at, ROWS), :] = high
            rl[pl.ds(at, ROWS), :] = low
    product = three_pass(split(a_ref[...]), (xh[...], xl[...]), ((1,), (0,)))
    for block in range(N_COL):
        y_all[block] = product[block * ROWS : (block + 1) * ROWS]
    high, low = split(product)
    rows_dims = ((0,), (0,))
    one = (rh[:, :WIDTH], rl[:, :WIDTH])
    two = (rh[:, WIDTH:], rl[:, WIDTH:])
    from_one = three_pass(one, (high, low), rows_dims)
    w_all[0:WIDTH, :] = from_one[:, :WIDTH]
    w_all[WIDTH : 2 * WIDTH, :] = from_one[:, WIDTH:]
    w_all[2 * WIDTH :, :] = three_pass(two, (high[:, WIDTH:], low[:, WIDTH:]), rows_dims)
    half = 3 * WIDTH // 2
    w_keep[...] = w_all[pl.ds(pl.multiple_of(k * half, 128), half), :]
    w_send[...] = w_all[pl.ds(pl.multiple_of((1 - k) * half, 128), half), :]
    for step in range(N_X):
        x = lax.rem(column + step, N_X)
        y_keep[step] = y_all[x * N_K + k]
        y_send[step] = y_all[x * N_K + 1 - k]


def product_and_grams(place, ancestor, gathered, own, other):
    f32, bf16 = jnp.float32, jnp.bfloat16
    half = 3 * WIDTH // 2
    wide = 2 * WIDTH
    vmem = pl.BlockSpec(memory_space=pltpu.VMEM)
    return pl.pallas_call(
        product_kernel,
        in_specs=[pl.BlockSpec(memory_space=pltpu.SMEM)] + [vmem] * 7,
        out_specs=[vmem] * 4,
        out_shape=[
            jax.ShapeDtypeStruct((half, WIDTH), f32),
            jax.ShapeDtypeStruct((half, WIDTH), f32),
            jax.ShapeDtypeStruct((N_X, ROWS, wide), f32),
            jax.ShapeDtypeStruct((N_X, ROWS, wide), f32),
        ],
        scratch_shapes=[
            pltpu.VMEM((1536, wide), bf16),
            pltpu.VMEM((1536, wide), bf16),
            pltpu.VMEM((384, wide), bf16),
            pltpu.VMEM((384, wide), bf16),
            pltpu.VMEM((3 * WIDTH, WIDTH), f32),
            pltpu.VMEM((N_COL, ROWS, wide), f32),
        ],
        compiler_params=pltpu.CompilerParams(vmem_limit_bytes=48 * 1024 * 1024),
        name="product_and_grams",
    )(place, ancestor, *gathered, own, other)


def at_owner(value, axis):
    count = lax.axis_size(axis)
    parts = value.reshape(count, value.shape[0] // count, *value.shape[1:])
    return lax.all_to_all(parts, axis, 0, 0, tiled=True)


def copies_of(value, axis):
    copies = jnp.broadcast_to(value[None], (lax.axis_size(axis), *value.shape))
    return lax.all_to_all(copies, axis, 0, 0, tiled=True)


def selection(tile_owner):
    tile_count = tile_owner.shape[0]
    owner = tile_owner[:, 0]
    order = jnp.arange(tile_count)
    same = (owner[:, None] == owner[None, :]) & (order[None, :] < order[:, None])
    rank = jnp.sum(same.astype(jnp.int32), axis=1)
    return (
        (owner[None, None, :] == jnp.arange(N_COL)[:, None, None])
        & (rank[None, None, :] == jnp.arange(CAP)[None, :, None])
    ).astype(jnp.float32)


def deliver(values, select):
    tile_count = select.shape[2]
    tile_rows = values.shape[0] // tile_count
    all_tiles = values.reshape(tile_count, tile_rows, values.shape[1])
    outgoing = jnp.einsum("cks,srb->ckrb", select, all_tiles, precision=lax.Precision.HIGHEST)
    incoming = lax.all_to_all(outgoing, COL, split_axis=0, concat_axis=0, tiled=True)
    return incoming.reshape(N_COL * CAP, tile_rows, values.shape[1])


def local(
    ancestor_inverse,
    panel_one,
    struct_one,
    lower_one,
    panel_two,
    struct_two,
    panel_above,
    lower_two,
    tile_owner,
):
    start = (lax.axis_index(ROW) * N_COL + lax.axis_index(COL)) * ROWS
    mask_one = row_mask(struct_one, start, ROWS)
    mask_two = row_mask(struct_two, start, ROWS)
    panels = jnp.concatenate([panel_one * mask_one, panel_two * mask_two], axis=1)
    block = lax.ppermute(panels, ROW_COL, to_column(0))
    far_block = lax.ppermute(panels, ROW_COL, to_column(2))
    own_core = lax.all_gather(panels, "col_0", axis=0)
    next_core = lax.ppermute(own_core, ROW_COL, other_core())
    block, far_block, own_core = lax.optimization_barrier((block, far_block, own_core))
    gathered = lax.all_gather(block, "row_1", axis=0, tiled=True)
    above = lax.ppermute(gathered, ROW_COL, along_y(-1))
    below = lax.ppermute(gathered, ROW_COL, along_y(1))
    far_block, _ = lax.optimization_barrier((far_block, gathered))
    far = lax.all_gather(far_block, "row_1", axis=0, tiled=True)
    place = jnp.stack([lax.axis_index(name) for name in ("row_0", "col_0", "col_1")])
    place = place.astype(jnp.int32)
    w_keep, w_send, y_keep, y_send = product_and_grams(
        place, ancestor_inverse, (gathered, above, far, below), own_core, next_core
    )
    w_own = w_keep + lax.ppermute(w_send, ROW_COL, other_core())
    y_send, w_own = lax.optimization_barrier((y_send, w_own))
    y_own = y_keep + lax.ppermute(y_send, ROW_COL, other_core())
    w_part = jnp.sum(at_owner(w_own, PLANE), axis=0)
    rows = y_own[0]
    for step in range(1, N_X):
        rows = rows + lax.ppermute(y_own[step], ROW_COL, along_x(step))
    w_part = jnp.sum(copies_of(w_part, "row_1"), axis=0)
    w_half = copies_of(w_part, PLANE).reshape(w_own.shape)
    w_other = lax.ppermute(w_half, ROW_COL, other_core())
    first = lax.axis_index("col_1") == 0
    grams = jnp.concatenate(
        [jnp.where(first, w_half, w_other), jnp.where(first, w_other, w_half)], axis=0
    )
    w_one, w_cross, w_two = grams[:WIDTH], grams[WIDTH : 2 * WIDTH], grams[2 * WIDTH :]
    diag_one = dot(lower_one, lower_one, ((0,), (0,))) + w_one
    cross_two = w_cross - dot(diag_one, panel_above)
    diag_two = (
        dot(lower_two, lower_two, ((0,), (0,)))
        + w_two
        - dot(w_cross, panel_above, ((0,), (0,)))
        - dot(panel_above, cross_two, ((0,), (0,)))
    )
    inverse_one = -rows[:, :WIDTH] * mask_one
    inverse_two = -(rows[:, WIDTH:] + dot(inverse_one, panel_above)) * mask_two
    inverses = lax.ppermute(
        jnp.concatenate([inverse_one, inverse_two], axis=1), ROW_COL, moves(result_place)
    )
    inverse_one, inverse_two = inverses[:, :WIDTH], inverses[:, WIDTH:]
    inverse_two, _ = lax.optimization_barrier((inverse_two, w_part))
    delivered = deliver(inverse_two, selection(tile_owner))
    return (inverse_one, diag_one, cross_two, diag_two, delivered)


def solution(mesh):
    finer = Mesh(mesh.devices.reshape(4, 8, 4, 2), ("row_0", "row_1", "col_0", "col_1"))
    return jax.shard_map(
        local,
        mesh=finer,
        in_specs=(
            P(ROW, COL),
            P(ROW_COL, None),
            P(),
            P(),
            P(ROW_COL, None),
            P(),
            P(),
            P(),
            P(COL_ROW, None),
        ),
        out_specs=(P(COL_ROW, None), P(), P(), P(), P(ROW_COL, None, None)),
        check_vma=False,
    )
```

```python
import jax
import jax.numpy as jnp
from jax import lax
from jax.experimental import pallas as pl
from jax.experimental.pallas import tpu as pltpu
from jax.sharding import Mesh
from jax.sharding import PartitionSpec as P

CAP = 2
COL = ("col_0", "col_1")
ROW = ("row_0", "row_1")
ROW_COL = ROW + COL
COL_ROW = COL + ROW
PLANE = ("row_0", "col_0")
N_Y, N_Z, N_X, N_K = 4, 8, 4, 2
N_ROW, N_COL = N_Y * N_Z, N_X * N_K
ROWS = 48
WIDTH = 256
TILES, TILE_ROWS = 6, 8
SMALL = pltpu.CompilerParams(vmem_limit_bytes=6 * 1024 * 1024)
SMEM = pl.BlockSpec(memory_space=pltpu.SMEM)
VMEM = pl.BlockSpec(memory_space=pltpu.VMEM)


def device(y, z, x, k):
    return ((y * N_Z + z) * N_X + x) * N_K + k


def moves(place):
    return [
        (device(y, z, x, k), device(*place(y, z, x, k)))
        for y in range(N_Y)
        for z in range(N_Z)
        for x in range(N_X)
        for k in range(N_K)
    ]


def to_column(step):
    return moves(lambda y, z, x, k: ((x + step) % N_Y, 2 * (z % 4) + k, y, z // 4))


def result_place(y, z, x, k):
    column, row = divmod((y * N_Z + z) * N_COL + x * N_K + k, N_ROW)
    return (row // N_Z, row % N_Z, column // N_K, column % N_K)


def along_y(step):
    return moves(lambda y, z, x, k: ((y + step) % N_Y, z, x, k))


def along_x(step):
    return moves(lambda y, z, x, k: (y, z, (x + step) % N_X, k))


def other_core():
    return moves(lambda y, z, x, k: (y, z, x, 1 - k))


def mask_kernel(start, one_ref, two_ref, panel_one, panel_two, panels, masks):
    rows = start[0] + lax.broadcasted_iota(jnp.int32, (ROWS, 128), 0)
    for part, (listed, panel) in enumerate(((one_ref, panel_one), (two_ref, panel_two))):
        hit = jnp.zeros((ROWS, 128), jnp.float32)
        for line in range(listed.shape[0]):
            hit = jnp.where(listed[line : line + 1, :] == rows, 1.0, hit)
        mask = jnp.broadcast_to(jnp.max(hit, axis=1, keepdims=True), (ROWS, WIDTH))
        columns = slice(part * WIDTH, (part + 1) * WIDTH)
        masks[:, columns] = mask
        panels[:, columns] = panel[...] * mask


def masked_panels(start, struct_one, struct_two, panel_one, panel_two):
    shape = jax.ShapeDtypeStruct((ROWS, 2 * WIDTH), jnp.float32)
    return pl.pallas_call(
        mask_kernel,
        in_specs=[SMEM] + [VMEM] * 4,
        out_specs=[VMEM] * 2,
        out_shape=[shape, shape],
        compiler_params=SMALL,
        name="masked_panels",
    )(start, struct_one.reshape(-1, 128), struct_two.reshape(-1, 128), panel_one, panel_two)


def dot(left, right, dims=((1,), (0,)), precision=lax.Precision.HIGHEST):
    return lax.dot_general(
        left, right, (dims, ((), ())), precision=precision, preferred_element_type=jnp.float32
    )


def split(value):
    high = value.astype(jnp.bfloat16)
    return high, (value - high.astype(jnp.float32)).astype(jnp.bfloat16)


def three_pass(left, right, dims):
    (a, b), (c, d) = left, right

    def one(p, q):
        return lax.dot_general(p, q, (dims, ((), ())), preferred_element_type=jnp.float32)

    return one(a, c) + (one(a, d) + one(b, c))


def product_kernel(
    place, a_ref, g0_ref, g1_ref, g2_ref, g3_ref, r0_ref, r1_ref, r2_ref, r3_ref,
    w_keep, w_send, y_keep, y_send, xh, xl, rh, rl, w_all, y_all,
):
    y, column, k = place[0], place[1], place[2]
    for step, g_ref in enumerate((g0_ref, g1_ref, g2_ref, g3_ref)):
        x = lax.rem(y + step, N_X)
        for q in range(4):
            high, low = split(g_ref[pl.ds(q * 96, 96), :])
            at = pl.multiple_of(q * 384 + x * 96, 32)
            xh[pl.ds(at, 96), :] = high
            xl[pl.ds(at, 96), :] = low
    for step, r_ref in enumerate((r0_ref, r1_ref, r2_ref, r3_ref)):
        x = lax.rem(column + N_X - step, N_X)
        for part, core in ((0, k), (1, 1 - k)):
            high, low = split(r_ref[part])
            at = pl.multiple_of((x * N_K + core) * ROWS, 16)
            rh[pl.ds(at, ROWS), :] = high
            rl[pl.ds(at, ROWS), :] = low
    product = three_pass(split(a_ref[...]), (xh[...], xl[...]), ((1,), (0,)))
    for block in range(N_COL):
        y_all[block] = product[block * ROWS : (block + 1) * ROWS]
    high, low = split(product)
    rows_dims = ((0,), (0,))
    one = (rh[:, :WIDTH], rl[:, :WIDTH])
    two = (rh[:, WIDTH:], rl[:, WIDTH:])
    from_one = three_pass(one, (high, low), rows_dims)
    w_all[0:WIDTH, :] = from_one[:, :WIDTH]
    w_all[WIDTH : 2 * WIDTH, :] = from_one[:, WIDTH:]
    w_all[2 * WIDTH :, :] = three_pass(two, (high[:, WIDTH:], low[:, WIDTH:]), rows_dims)
    half = 3 * WIDTH // 2
    w_keep[...] = w_all[pl.ds(pl.multiple_of(k * half, 128), half), :]
    w_send[...] = w_all[pl.ds(pl.multiple_of((1 - k) * half, 128), half), :]
    for step in range(N_X):
        x = lax.rem(column + step, N_X)
        y_keep[step] = y_all[x * N_K + k]
        y_send[step] = y_all[x * N_K + 1 - k]


def product_and_grams(place, ancestor, gathered, row_panels):
    f32, bf16 = jnp.float32, jnp.bfloat16
    half = 3 * WIDTH // 2
    wide = 2 * WIDTH
    return pl.pallas_call(
        product_kernel,
        in_specs=[SMEM] + [VMEM] * 9,
        out_specs=[VMEM] * 4,
        out_shape=[
            jax.ShapeDtypeStruct((half, WIDTH), f32),
            jax.ShapeDtypeStruct((half, WIDTH), f32),
            jax.ShapeDtypeStruct((N_X, ROWS, wide), f32),
            jax.ShapeDtypeStruct((N_X, ROWS, wide), f32),
        ],
        scratch_shapes=[
            pltpu.VMEM((1536, wide), bf16),
            pltpu.VMEM((1536, wide), bf16),
            pltpu.VMEM((384, wide), bf16),
            pltpu.VMEM((384, wide), bf16),
            pltpu.VMEM((3 * WIDTH, WIDTH), f32),
            pltpu.VMEM((N_COL, ROWS, wide), f32),
        ],
        compiler_params=pltpu.CompilerParams(vmem_limit_bytes=24 * 1024 * 1024),
        name="product_and_grams",
    )(place, ancestor, *gathered, *row_panels)


def at_owner(value, axis):
    count = lax.axis_size(axis)
    parts = value.reshape(count, value.shape[0] // count, *value.shape[1:])
    return lax.all_to_all(parts, axis, 0, 0, tiled=True)


def copies_of(value, axis):
    copies = jnp.broadcast_to(value[None], (lax.axis_size(axis), *value.shape))
    return lax.all_to_all(copies, axis, 0, 0, tiled=True)


def inverse_kernel(y0, y1, y2, y3, masks, above, out):
    rows = (y0[...] + y1[...]) + (y2[...] + y3[...])
    one = -rows[:, :WIDTH] * masks[:, :WIDTH]
    out[:, :WIDTH] = one
    out[:, WIDTH:] = -(rows[:, WIDTH:] + dot(one, above[...])) * masks[:, WIDTH:]


def inverse_rows(parts, masks, panel_above):
    return pl.pallas_call(
        inverse_kernel,
        in_specs=[VMEM] * 6,
        out_specs=VMEM,
        out_shape=jax.ShapeDtypeStruct((ROWS, 2 * WIDTH), jnp.float32),
        compiler_params=SMALL,
        name="inverse_rows",
    )(*parts, masks, panel_above)


def pick_kernel(place, owner, rows, one, keep, send):
    column, k = place[1], place[2]
    one[...] = rows[:, :WIDTH]
    keep[...] = jnp.zeros(keep.shape, jnp.float32)
    send[...] = jnp.zeros(send.shape, jnp.float32)
    for tile in range(TILES):
        mine = owner[tile]
        rank = jnp.int32(0)
        for earlier in range(tile):
            rank = rank + jnp.where(owner[earlier] == mine, 1, 0)
        rank = jnp.minimum(rank, CAP - 1)
        step = lax.rem(lax.div(mine, N_K) + N_X - column, N_X)
        core = lax.rem(mine, N_K)
        values = rows[tile * TILE_ROWS : (tile + 1) * TILE_ROWS, WIDTH:]

        @pl.when(core == k)
        def _():
            keep[step * CAP + rank] = values

        @pl.when(core != k)
        def _():
            send[step * CAP + rank] = values


def pick_tiles(place, tile_owner, rows):
    tiles = jax.ShapeDtypeStruct((N_X * CAP, TILE_ROWS, WIDTH), jnp.float32)
    return pl.pallas_call(
        pick_kernel,
        in_specs=[SMEM, SMEM, VMEM],
        out_specs=[VMEM] * 3,
        out_shape=[jax.ShapeDtypeStruct((ROWS, WIDTH), jnp.float32), tiles, tiles],
        compiler_params=SMALL,
        name="pick_tiles",
    )(place, tile_owner.reshape(-1), rows)


def slots_kernel(place, p0, p1, p2, p3, out):
    column, k = place[1], place[2]
    for step, part in enumerate((p0, p1, p2, p3)):
        x = lax.rem(column + N_X - step, N_X)
        for source, core in ((0, k), (1, 1 - k)):
            for slot in range(CAP):
                out[(x * N_K + core) * CAP + slot] = part[source, slot]


def fill_slots(place, parts):
    return pl.pallas_call(
        slots_kernel,
        in_specs=[SMEM] + [VMEM] * 4,
        out_specs=VMEM,
        out_shape=jax.ShapeDtypeStruct((N_COL * CAP, TILE_ROWS, WIDTH), jnp.float32),
        compiler_params=SMALL,
        name="fill_slots",
    )(place, *parts)


def deliver(place, tile_owner, rows):
    inverse_one, keep, send = pick_tiles(place, tile_owner, rows)
    shape = (N_X, CAP, TILE_ROWS, WIDTH)
    arrived = lax.ppermute(send, ROW_COL, other_core())
    pairs = jnp.stack([keep.reshape(shape), arrived.reshape(shape)], axis=1)
    parts = [pairs[0]]
    for step in range(1, N_X):
        parts.append(lax.ppermute(pairs[step], ROW_COL, along_x(step)))
    return inverse_one, fill_slots(place, parts)


def final_kernel(place, half, other, square_one, square_two, above, diag_one, cross_two, diag_two, w):
    rows = half.shape[0]
    first = pl.multiple_of(place[2] * rows, 128)
    second = pl.multiple_of((1 - place[2]) * rows, 128)
    w[pl.ds(first, rows), :] = half[...]
    w[pl.ds(second, rows), :] = other[...]
    w_cross = w[WIDTH : 2 * WIDTH]
    rows_dims = ((0,), (0,))
    one = square_one[...] + w[:WIDTH]
    cross = w_cross - dot(one, above[...])
    diag_one[...] = one
    cross_two[...] = cross
    twice = dot(w_cross, above[...], rows_dims) + dot(above[...], cross, rows_dims)
    diag_two[...] = square_two[...] + w[2 * WIDTH :] - twice


def final_blocks(place, half, other, square_one, square_two, panel_above):
    block = jax.ShapeDtypeStruct((WIDTH, WIDTH), jnp.float32)
    return pl.pallas_call(
        final_kernel,
        in_specs=[SMEM] + [VMEM] * 5,
        out_specs=[VMEM] * 3,
        out_shape=[block] * 3,
        scratch_shapes=[pltpu.VMEM((3 * WIDTH, WIDTH), jnp.float32)],
        compiler_params=SMALL,
        name="final_blocks",
    )(place, half, other, square_one, square_two, panel_above)


def local(
    ancestor_inverse,
    panel_one,
    struct_one,
    lower_one,
    panel_two,
    struct_two,
    panel_above,
    lower_two,
    tile_owner,
):
    start = (lax.axis_index(ROW) * N_COL + lax.axis_index(COL)) * ROWS
    place = jnp.stack([lax.axis_index(name) for name in ("row_0", "col_0", "col_1")])
    place = place.astype(jnp.int32)
    panels, masks = masked_panels(
        start.astype(jnp.int32)[None], struct_one, struct_two, panel_one, panel_two
    )
    block = lax.ppermute(panels, ROW_COL, to_column(0))
    far_block = lax.ppermute(panels, ROW_COL, to_column(2))
    sibling = lax.ppermute(panels, ROW_COL, other_core())
    block, far_block, sibling = lax.optimization_barrier((block, far_block, sibling))
    pair = jnp.stack([panels, sibling])
    gathered = lax.all_gather(block, "row_1", axis=0, tiled=True)
    above = lax.ppermute(gathered, ROW_COL, along_y(-1))
    below = lax.ppermute(gathered, ROW_COL, along_y(1))
    far_block, pair, _ = lax.optimization_barrier((far_block, pair, gathered))
    row_panels = [pair]
    for step in range(1, N_X):
        row_panels.append(lax.ppermute(pair, ROW_COL, along_x(step)))
    far = lax.all_gather(far_block, "row_1", axis=0, tiled=True)
    w_keep, w_send, y_keep, y_send = product_and_grams(
        place, ancestor_inverse, (gathered, above, far, below), row_panels
    )
    w_own = w_keep + lax.ppermute(w_send, ROW_COL, other_core())
    y_send, w_own = lax.optimization_barrier((y_send, w_own))
    y_own = y_keep + lax.ppermute(y_send, ROW_COL, other_core())
    y_parts = [y_own[0]]
    for step in range(1, N_X):
        y_parts.append(lax.ppermute(y_own[step], ROW_COL, along_x(step)))
    w_part = jnp.sum(at_owner(w_own, PLANE), axis=0)
    w_part, y_parts = lax.optimization_barrier((w_part, y_parts))
    w_part = jnp.sum(copies_of(w_part, "row_1"), axis=0)
    inverses = inverse_rows(y_parts, masks, panel_above)
    w_part, _ = lax.optimization_barrier((w_part, inverses))
    w_half = copies_of(w_part, PLANE).reshape(w_own.shape)
    w_other = lax.ppermute(w_half, ROW_COL, other_core())
    inverses = lax.ppermute(inverses, ROW_COL, moves(result_place))
    inverse_one, delivered = deliver(place, tile_owner, inverses)
    square_one = dot(lower_one, lower_one, ((0,), (0,)))
    square_two = dot(lower_two, lower_two, ((0,), (0,)))
    diag_one, cross_two, diag_two = final_blocks(
        place, w_half, w_other, square_one, square_two, panel_above
    )
    return (inverse_one, diag_one, cross_two, diag_two, delivered)


def solution(mesh):
    finer = Mesh(mesh.devices.reshape(4, 8, 4, 2), ("row_0", "row_1", "col_0", "col_1"))
    return jax.shard_map(
        local,
        mesh=finer,
        in_specs=(
            P(ROW, COL),
            P(ROW_COL, None),
            P(),
            P(),
            P(ROW_COL, None),
            P(),
            P(),
            P(),
            P(COL_ROW, None),
        ),
        out_specs=(P(COL_ROW, None), P(), P(), P(), P(ROW_COL, None, None)),
        check_vma=False,
    )
```

```python
import jax
import jax.numpy as jnp
from jax import lax
from jax.experimental import pallas as pl
from jax.experimental.pallas import tpu as pltpu
from jax.sharding import Mesh
from jax.sharding import PartitionSpec as P

CAP = 2
COL = ("col_0", "col_1")
ROW = ("row_0", "row_1")
ROW_COL = ROW + COL
COL_ROW = COL + ROW
PLANE = ("row_0", "col_0")
N_Y, N_Z, N_X, N_K = 4, 8, 4, 2
N_ROW, N_COL = N_Y * N_Z, N_X * N_K
ROWS = 48
WIDTH = 256
TILES, TILE_ROWS = 6, 8
SMALL = pltpu.CompilerParams(vmem_limit_bytes=6 * 1024 * 1024)
SMEM = pl.BlockSpec(memory_space=pltpu.SMEM)
VMEM = pl.BlockSpec(memory_space=pltpu.VMEM)


def device(y, z, x, k):
    return ((y * N_Z + z) * N_X + x) * N_K + k


def moves(place):
    return [
        (device(y, z, x, k), device(*place(y, z, x, k)))
        for y in range(N_Y)
        for z in range(N_Z)
        for x in range(N_X)
        for k in range(N_K)
    ]


def to_column(step):
    return moves(lambda y, z, x, k: ((x + step) % N_Y, 2 * (z % 4) + k, y, z // 4))


def result_place(y, z, x, k):
    column, row = divmod((y * N_Z + z) * N_COL + x * N_K + k, N_ROW)
    return (row // N_Z, row % N_Z, column // N_K, column % N_K)


def along_y(step):
    return moves(lambda y, z, x, k: ((y + step) % N_Y, z, x, k))


def along_z(step):
    return moves(lambda y, z, x, k: (y, (z + step) % N_Z, x, k))


def along_x(step):
    return moves(lambda y, z, x, k: (y, z, (x + step) % N_X, k))


def other_core():
    return moves(lambda y, z, x, k: (y, z, x, 1 - k))


def mask_kernel(
    start, one_hbm, two_hbm, panel_one_hbm, panel_two_hbm, panels, masks,
    one_ref, two_ref, panel_one, panel_two, sems,
):
    pairs = (
        (one_hbm, one_ref),
        (two_hbm, two_ref),
        (panel_one_hbm, panel_one),
        (panel_two_hbm, panel_two),
    )
    copies = [
        pltpu.make_async_copy(source, target, sems.at[i])
        for i, (source, target) in enumerate(pairs)
    ]
    for copy in copies:
        copy.start()
    for copy in copies:
        copy.wait()
    rows = start[0] + lax.broadcasted_iota(jnp.int32, (ROWS, 128), 0)
    for part, (listed, panel) in enumerate(((one_ref, panel_one), (two_ref, panel_two))):
        hit = jnp.zeros((ROWS, 128), jnp.float32)
        for line in range(listed.shape[0]):
            hit = jnp.where(listed[line : line + 1, :] == rows, 1.0, hit)
        mask = jnp.broadcast_to(jnp.max(hit, axis=1, keepdims=True), (ROWS, WIDTH))
        columns = slice(part * WIDTH, (part + 1) * WIDTH)
        masks[:, columns] = mask
        panels[:, columns] = panel[...] * mask


def masked_panels(start, struct_one, struct_two, panel_one, panel_two):
    shape = jax.ShapeDtypeStruct((ROWS, 2 * WIDTH), jnp.float32)
    one, two = struct_one.reshape(-1, 128), struct_two.reshape(-1, 128)
    fetched = [
        pltpu.with_memory_space_constraint(value, pltpu.HBM)
        for value in (one, two, panel_one, panel_two)
    ]
    return pl.pallas_call(
        mask_kernel,
        in_specs=[SMEM] + [pl.BlockSpec(memory_space=pltpu.HBM)] * 4,
        out_specs=[VMEM] * 2,
        out_shape=[shape, shape],
        scratch_shapes=[
            pltpu.VMEM(one.shape, jnp.int32),
            pltpu.VMEM(two.shape, jnp.int32),
            pltpu.VMEM((ROWS, WIDTH), jnp.float32),
            pltpu.VMEM((ROWS, WIDTH), jnp.float32),
            pltpu.SemaphoreType.DMA((4,)),
        ],
        compiler_params=SMALL,
        name="masked_panels",
    )(start, *fetched)


def dot(left, right, dims=((1,), (0,)), precision=lax.Precision.HIGHEST):
    return lax.dot_general(
        left, right, (dims, ((), ())), precision=precision, preferred_element_type=jnp.float32
    )


def split(value):
    high = value.astype(jnp.bfloat16)
    return high, (value - high.astype(jnp.float32)).astype(jnp.bfloat16)


def three_pass(left, right, dims):
    (a, b), (c, d) = left, right

    def one(p, q):
        return lax.dot_general(p, q, (dims, ((), ())), preferred_element_type=jnp.float32)

    return one(a, c) + (one(a, d) + one(b, c))


RING = (0, -1, 1, -2, 2, -3, 3)
BATCHES = ((0, -1, 1, -2, 2), (-3, 3), (4,))


def product_kernel(place, a_ref, *refs):
    ring, (last_own, last_far) = refs[:7], refs[7:9]
    above, below = refs[9:12], refs[12:15]
    r0_ref, r1_ref, r2_ref, r3_ref = refs[15:19]
    w_keep, w_send, y_keep, y_send, xh, xl, rh, rl, w_all, y_all = refs[19:]
    y, column, k, z = place[0], place[1], place[2], place[3]

    def put(step, offset, values):
        x = lax.rem(y + step, N_X)
        at = lax.rem(z + N_Z + offset, N_Z)
        first = lax.div(at, 2) * 384 + x * 96 + lax.rem(at, 2) * ROWS
        first = pl.multiple_of(first, 16)
        high, low = split(values)
        xh[pl.ds(first, ROWS), :] = high
        xl[pl.ds(first, ROWS), :] = low

    for offset, ref in zip(RING, ring):
        put(0, offset, ref[:ROWS])
        put(2, offset, ref[ROWS:])
    put(0, 4, last_own[...])
    put(2, 4, last_far[...])
    for step, batches in ((1, above), (3, below)):
        for offsets, ref in zip(BATCHES, batches):
            for i, offset in enumerate(offsets):
                put(step, offset, ref[i * ROWS : (i + 1) * ROWS])
    for step, r_ref in enumerate((r0_ref, r1_ref, r2_ref, r3_ref)):
        x = lax.rem(column + N_X - step, N_X)
        for part, core in ((0, k), (1, 1 - k)):
            high, low = split(r_ref[part])
            at = pl.multiple_of((x * N_K + core) * ROWS, 16)
            rh[pl.ds(at, ROWS), :] = high
            rl[pl.ds(at, ROWS), :] = low
    product = three_pass(split(a_ref[...]), (xh[...], xl[...]), ((1,), (0,)))
    for block in range(N_COL):
        y_all[block] = product[block * ROWS : (block + 1) * ROWS]
    high, low = split(product)
    rows_dims = ((0,), (0,))
    one = (rh[:, :WIDTH], rl[:, :WIDTH])
    two = (rh[:, WIDTH:], rl[:, WIDTH:])
    from_one = three_pass(one, (high, low), rows_dims)
    w_all[0:WIDTH, :] = from_one[:, :WIDTH]
    w_all[WIDTH : 2 * WIDTH, :] = from_one[:, WIDTH:]
    w_all[2 * WIDTH :, :] = three_pass(two, (high[:, WIDTH:], low[:, WIDTH:]), rows_dims)
    half = 3 * WIDTH // 2
    w_keep[...] = w_all[pl.ds(pl.multiple_of(k * half, 128), half), :]
    w_send[...] = w_all[pl.ds(pl.multiple_of((1 - k) * half, 128), half), :]
    for step in range(N_X):
        x = lax.rem(column + step, N_X)
        y_keep[step] = y_all[x * N_K + k]
        y_send[step] = y_all[x * N_K + 1 - k]


def product_and_grams(place, ancestor, gathered):
    f32, bf16 = jnp.float32, jnp.bfloat16
    half = 3 * WIDTH // 2
    wide = 2 * WIDTH
    return pl.pallas_call(
        product_kernel,
        in_specs=[SMEM] + [VMEM] * 20,
        out_specs=[VMEM] * 4,
        out_shape=[
            jax.ShapeDtypeStruct((half, WIDTH), f32),
            jax.ShapeDtypeStruct((half, WIDTH), f32),
            jax.ShapeDtypeStruct((N_X, ROWS, wide), f32),
            jax.ShapeDtypeStruct((N_X, ROWS, wide), f32),
        ],
        scratch_shapes=[
            pltpu.VMEM((1536, wide), bf16),
            pltpu.VMEM((1536, wide), bf16),
            pltpu.VMEM((384, wide), bf16),
            pltpu.VMEM((384, wide), bf16),
            pltpu.VMEM((3 * WIDTH, WIDTH), f32),
            pltpu.VMEM((N_COL, ROWS, wide), f32),
        ],
        compiler_params=pltpu.CompilerParams(vmem_limit_bytes=24 * 1024 * 1024),
        name="product_and_grams",
    )(place, ancestor, *gathered)


def at_owner(value, axis):
    count = lax.axis_size(axis)
    parts = value.reshape(count, value.shape[0] // count, *value.shape[1:])
    return lax.all_to_all(parts, axis, 0, 0, tiled=True)


def copies_of(value, axis):
    copies = jnp.broadcast_to(value[None], (lax.axis_size(axis), *value.shape))
    return lax.all_to_all(copies, axis, 0, 0, tiled=True)


def inverse_kernel(y0, y1, y2, y3, masks, above, out):
    rows = (y0[...] + y1[...]) + (y2[...] + y3[...])
    one = -rows[:, :WIDTH] * masks[:, :WIDTH]
    out[:, :WIDTH] = one
    out[:, WIDTH:] = -(rows[:, WIDTH:] + dot(one, above[...])) * masks[:, WIDTH:]


def inverse_rows(parts, masks, panel_above):
    return pl.pallas_call(
        inverse_kernel,
        in_specs=[VMEM] * 6,
        out_specs=VMEM,
        out_shape=jax.ShapeDtypeStruct((ROWS, 2 * WIDTH), jnp.float32),
        compiler_params=SMALL,
        name="inverse_rows",
    )(*parts, masks, panel_above)


def pick_kernel(place, owner, rows, one, keep, send):
    column, k = place[1], place[2]
    one[...] = rows[:, :WIDTH]
    keep[...] = jnp.zeros(keep.shape, jnp.float32)
    send[...] = jnp.zeros(send.shape, jnp.float32)
    for tile in range(TILES):
        mine = owner[tile]
        rank = jnp.int32(0)
        for earlier in range(tile):
            rank = rank + jnp.where(owner[earlier] == mine, 1, 0)
        rank = jnp.minimum(rank, CAP - 1)
        step = lax.rem(lax.div(mine, N_K) + N_X - column, N_X)
        core = lax.rem(mine, N_K)
        values = rows[tile * TILE_ROWS : (tile + 1) * TILE_ROWS, WIDTH:]

        @pl.when(core == k)
        def _():
            keep[step * CAP + rank] = values

        @pl.when(core != k)
        def _():
            send[step * CAP + rank] = values


def pick_tiles(place, tile_owner, rows):
    tiles = jax.ShapeDtypeStruct((N_X * CAP, TILE_ROWS, WIDTH), jnp.float32)
    return pl.pallas_call(
        pick_kernel,
        in_specs=[SMEM, SMEM, VMEM],
        out_specs=[VMEM] * 3,
        out_shape=[jax.ShapeDtypeStruct((ROWS, WIDTH), jnp.float32), tiles, tiles],
        compiler_params=SMALL,
        name="pick_tiles",
    )(place, tile_owner.reshape(-1), rows)


def slots_kernel(place, p0, p1, p2, p3, out):
    column, k = place[1], place[2]
    for step, part in enumerate((p0, p1, p2, p3)):
        x = lax.rem(column + N_X - step, N_X)
        for source, core in ((0, k), (1, 1 - k)):
            for slot in range(CAP):
                out[(x * N_K + core) * CAP + slot] = part[source, slot]


def fill_slots(place, parts):
    return pl.pallas_call(
        slots_kernel,
        in_specs=[SMEM] + [VMEM] * 4,
        out_specs=VMEM,
        out_shape=jax.ShapeDtypeStruct((N_COL * CAP, TILE_ROWS, WIDTH), jnp.float32),
        compiler_params=SMALL,
        name="fill_slots",
    )(place, *parts)


def deliver(place, keep, arrived):
    shape = (N_X, CAP, TILE_ROWS, WIDTH)
    pairs = jnp.stack([keep.reshape(shape), arrived.reshape(shape)], axis=1)
    parts = [pairs[0]]
    for step in range(1, N_X):
        parts.append(lax.ppermute(pairs[step], ROW_COL, along_x(step)))
    return fill_slots(place, parts)


def final_kernel(place, half, other, square_one, square_two, above, diag_one, cross_two, diag_two, w):
    rows = half.shape[0]
    first = pl.multiple_of(place[2] * rows, 128)
    second = pl.multiple_of((1 - place[2]) * rows, 128)
    w[pl.ds(first, rows), :] = half[...]
    w[pl.ds(second, rows), :] = other[...]
    w_cross = w[WIDTH : 2 * WIDTH]
    rows_dims = ((0,), (0,))
    one = square_one[...] + w[:WIDTH]
    cross = w_cross - dot(one, above[...])
    diag_one[...] = one
    cross_two[...] = cross
    twice = dot(w_cross, above[...], rows_dims) + dot(above[...], cross, rows_dims)
    diag_two[...] = square_two[...] + w[2 * WIDTH :] - twice


def final_blocks(place, half, other, square_one, square_two, panel_above):
    block = jax.ShapeDtypeStruct((WIDTH, WIDTH), jnp.float32)
    return pl.pallas_call(
        final_kernel,
        in_specs=[SMEM] + [VMEM] * 5,
        out_specs=[VMEM] * 3,
        out_shape=[block] * 3,
        scratch_shapes=[pltpu.VMEM((3 * WIDTH, WIDTH), jnp.float32)],
        compiler_params=SMALL,
        name="final_blocks",
    )(place, half, other, square_one, square_two, panel_above)


def local(
    ancestor_inverse,
    panel_one,
    struct_one,
    lower_one,
    panel_two,
    struct_two,
    panel_above,
    lower_two,
    tile_owner,
):
    start = (lax.axis_index(ROW) * N_COL + lax.axis_index(COL)) * ROWS
    place = jnp.stack([lax.axis_index(name) for name in ("row_0", "col_0", "col_1", "row_1")])
    place = place.astype(jnp.int32)
    panels, masks = masked_panels(
        start.astype(jnp.int32)[None], struct_one, struct_two, panel_one, panel_two
    )
    block = lax.ppermute(panels, ROW_COL, to_column(0))
    far_block = lax.ppermute(panels, ROW_COL, to_column(2))
    sibling = lax.ppermute(panels, ROW_COL, other_core())
    block, far_block, sibling = lax.optimization_barrier((block, far_block, sibling))
    pair = jnp.stack([panels, sibling])
    both = jnp.concatenate([block, far_block], axis=0)
    ring = [both]
    up = down = both
    for _ in range(3):
        up = lax.ppermute(up, ROW_COL, along_z(1))
        down = lax.ppermute(down, ROW_COL, along_z(-1))
        ring += [up, down]
    last_own = lax.ppermute(up[:ROWS], ROW_COL, along_z(1))
    last_far = lax.ppermute(down[ROWS:], ROW_COL, along_z(-1))
    batches = (
        jnp.concatenate([part[:ROWS] for part in ring[:5]], axis=0),
        jnp.concatenate([part[:ROWS] for part in ring[5:]], axis=0),
        last_own,
    )
    above = [lax.ppermute(batch, ROW_COL, along_y(-1)) for batch in batches]
    below = [lax.ppermute(batch, ROW_COL, along_y(1)) for batch in batches]
    row_panels = [pair]
    for step in range(1, N_X):
        row_panels.append(lax.ppermute(pair, ROW_COL, along_x(step)))
    w_keep, w_send, y_keep, y_send = product_and_grams(
        place,
        ancestor_inverse,
        (*ring, last_own, last_far, *above, *below, *row_panels),
    )
    w_own = w_keep + lax.ppermute(w_send, ROW_COL, other_core())
    y_send, w_own = lax.optimization_barrier((y_send, w_own))
    y_own = y_keep + lax.ppermute(y_send, ROW_COL, other_core())
    y_parts = [y_own[0]]
    for step in range(1, N_X):
        y_parts.append(lax.ppermute(y_own[step], ROW_COL, along_x(step)))
    w_part = jnp.sum(at_owner(w_own, PLANE), axis=0)
    inverses = inverse_rows(y_parts, masks, panel_above)
    w_part, inverses = lax.optimization_barrier((w_part, inverses))
    inverses = lax.ppermute(inverses, ROW_COL, moves(result_place))
    w_parts, inverses = lax.optimization_barrier((copies_of(w_part, "row_1"), inverses))
    w_half = copies_of(jnp.sum(w_parts, axis=0), PLANE).reshape(w_own.shape)
    inverse_one, keep, send = pick_tiles(place, tile_owner, inverses)
    arrived = lax.ppermute(send, ROW_COL, other_core())
    w_half, arrived = lax.optimization_barrier((w_half, arrived))
    w_other = lax.ppermute(w_half, ROW_COL, other_core())
    delivered = deliver(place, keep, arrived)
    square_one = dot(lower_one, lower_one, ((0,), (0,)))
    square_two = dot(lower_two, lower_two, ((0,), (0,)))
    diag_one, cross_two, diag_two = final_blocks(
        place, w_half, w_other, square_one, square_two, panel_above
    )
    return (inverse_one, diag_one, cross_two, diag_two, delivered)


def solution(mesh):
    finer = Mesh(mesh.devices.reshape(4, 8, 4, 2), ("row_0", "row_1", "col_0", "col_1"))
    return jax.shard_map(
        local,
        mesh=finer,
        in_specs=(
            P(ROW, COL),
            P(ROW_COL, None),
            P(),
            P(),
            P(ROW_COL, None),
            P(),
            P(),
            P(),
            P(COL_ROW, None),
        ),
        out_specs=(P(COL_ROW, None), P(), P(), P(), P(ROW_COL, None, None)),
        check_vma=False,
    )
```

```python
import jax
import jax.numpy as jnp
from jax import lax
from jax.experimental import pallas as pl
from jax.experimental.pallas import tpu as pltpu
from jax.sharding import Mesh
from jax.sharding import PartitionSpec as P

CAP = 2
COL = ("col_0", "col_1")
ROW = ("row_0", "row_1")
ROW_COL = ROW + COL
COL_ROW = COL + ROW
PLANE = ("row_0", "col_0")
N_Y, N_Z, N_X, N_K = 4, 8, 4, 2
N_ROW, N_COL = N_Y * N_Z, N_X * N_K
ROWS = 48
WIDTH = 256
TILES, TILE_ROWS = 6, 8
SMALL = pltpu.CompilerParams(vmem_limit_bytes=6 * 1024 * 1024)
SMEM = pl.BlockSpec(memory_space=pltpu.SMEM)
VMEM = pl.BlockSpec(memory_space=pltpu.VMEM)


def device(y, z, x, k):
    return ((y * N_Z + z) * N_X + x) * N_K + k


def moves(place):
    return [
        (device(y, z, x, k), device(*place(y, z, x, k)))
        for y in range(N_Y)
        for z in range(N_Z)
        for x in range(N_X)
        for k in range(N_K)
    ]


def to_column(step):
    return moves(lambda y, z, x, k: ((x + step) % N_Y, 2 * (z % 4) + k, y, z // 4))


def result_place(y, z, x, k):
    column, row = divmod((y * N_Z + z) * N_COL + x * N_K + k, N_ROW)
    return (row // N_Z, row % N_Z, column // N_K, column % N_K)


def along_y(step):
    return moves(lambda y, z, x, k: ((y + step) % N_Y, z, x, k))


def along_z(step):
    return moves(lambda y, z, x, k: (y, (z + step) % N_Z, x, k))


def along_x(step):
    return moves(lambda y, z, x, k: (y, z, (x + step) % N_X, k))


def other_core():
    return moves(lambda y, z, x, k: (y, z, x, 1 - k))


def mask_kernel(
    start, one_hbm, two_hbm, panel_one_hbm, panel_two_hbm, panels, masks,
    one_ref, two_ref, panel_one, panel_two, sems,
):
    pairs = (
        (one_hbm, one_ref),
        (two_hbm, two_ref),
        (panel_one_hbm, panel_one),
        (panel_two_hbm, panel_two),
    )
    copies = [
        pltpu.make_async_copy(source, target, sems.at[i])
        for i, (source, target) in enumerate(pairs)
    ]
    for copy in copies:
        copy.start()
    for copy in copies:
        copy.wait()
    rows = start[0] + lax.broadcasted_iota(jnp.int32, (ROWS, 128), 0)
    for part, (listed, panel) in enumerate(((one_ref, panel_one), (two_ref, panel_two))):
        hit = jnp.zeros((ROWS, 128), jnp.float32)
        for line in range(listed.shape[0]):
            hit = jnp.where(listed[line : line + 1, :] == rows, 1.0, hit)
        mask = jnp.broadcast_to(jnp.max(hit, axis=1, keepdims=True), (ROWS, WIDTH))
        columns = slice(part * WIDTH, (part + 1) * WIDTH)
        masks[:, columns] = mask
        panels[:, columns] = panel[...] * mask


def masked_panels(start, struct_one, struct_two, panel_one, panel_two):
    shape = jax.ShapeDtypeStruct((ROWS, 2 * WIDTH), jnp.float32)
    one, two = struct_one.reshape(-1, 128), struct_two.reshape(-1, 128)
    fetched = [
        pltpu.with_memory_space_constraint(value, pltpu.HBM)
        for value in (one, two, panel_one, panel_two)
    ]
    return pl.pallas_call(
        mask_kernel,
        in_specs=[SMEM] + [pl.BlockSpec(memory_space=pltpu.HBM)] * 4,
        out_specs=[VMEM] * 2,
        out_shape=[shape, shape],
        scratch_shapes=[
            pltpu.VMEM(one.shape, jnp.int32),
            pltpu.VMEM(two.shape, jnp.int32),
            pltpu.VMEM((ROWS, WIDTH), jnp.float32),
            pltpu.VMEM((ROWS, WIDTH), jnp.float32),
            pltpu.SemaphoreType.DMA((4,)),
        ],
        compiler_params=SMALL,
        name="masked_panels",
    )(start, *fetched)


def dot(left, right, dims=((1,), (0,)), precision=lax.Precision.HIGHEST):
    return lax.dot_general(
        left, right, (dims, ((), ())), precision=precision, preferred_element_type=jnp.float32
    )


def split(value):
    high = value.astype(jnp.bfloat16)
    return high, (value - high.astype(jnp.float32)).astype(jnp.bfloat16)


def three_pass(left, right, dims):
    (a, b), (c, d) = left, right

    def one(p, q):
        return lax.dot_general(p, q, (dims, ((), ())), preferred_element_type=jnp.float32)

    return one(a, c) + (one(a, d) + one(b, c))


RING = (0, -1, 1, -2, 2, -3, 3)
BATCHES = ((0, -1, 1, -2, 2), (-3, 3, 4))


def product_kernel(place, a_ref, *refs):
    ring, (last_own, last_far) = refs[:7], refs[7:9]
    above, below = refs[9:11], refs[11:13]
    r0_ref, r1_ref, r2_ref, r3_ref = refs[13:17]
    w_keep, w_send, y_keep, y_send, xh, xl, rh, rl, w_all, y_all = refs[17:]
    y, column, k, z = place[0], place[1], place[2], place[3]

    def put(step, offset, values):
        x = lax.rem(y + step, N_X)
        at = lax.rem(z + N_Z + offset, N_Z)
        first = lax.div(at, 2) * 384 + x * 96 + lax.rem(at, 2) * ROWS
        first = pl.multiple_of(first, 16)
        high, low = split(values)
        xh[pl.ds(first, ROWS), :] = high
        xl[pl.ds(first, ROWS), :] = low

    for offset, ref in zip(RING, ring):
        put(0, offset, ref[:ROWS])
        put(2, offset, ref[ROWS:])
    put(0, 4, last_own[...])
    put(2, 4, last_far[...])
    for step, batches in ((1, above), (3, below)):
        for offsets, ref in zip(BATCHES, batches):
            for i, offset in enumerate(offsets):
                put(step, offset, ref[i * ROWS : (i + 1) * ROWS])
    for step, r_ref in enumerate((r0_ref, r1_ref, r2_ref, r3_ref)):
        x = lax.rem(column + N_X - step, N_X)
        for part, core in ((0, k), (1, 1 - k)):
            high, low = split(r_ref[part])
            at = pl.multiple_of((x * N_K + core) * ROWS, 16)
            rh[pl.ds(at, ROWS), :] = high
            rl[pl.ds(at, ROWS), :] = low
    product = three_pass(split(a_ref[...]), (xh[...], xl[...]), ((1,), (0,)))
    for block in range(N_COL):
        y_all[block] = product[block * ROWS : (block + 1) * ROWS]
    high, low = split(product)
    rows_dims = ((0,), (0,))
    one = (rh[:, :WIDTH], rl[:, :WIDTH])
    two = (rh[:, WIDTH:], rl[:, WIDTH:])
    from_one = three_pass(one, (high, low), rows_dims)
    w_all[0:WIDTH, :] = from_one[:, :WIDTH]
    w_all[WIDTH : 2 * WIDTH, :] = from_one[:, WIDTH:]
    w_all[2 * WIDTH :, :] = three_pass(two, (high[:, WIDTH:], low[:, WIDTH:]), rows_dims)
    half = 3 * WIDTH // 2
    w_keep[...] = w_all[pl.ds(pl.multiple_of(k * half, 128), half), :]
    w_send[...] = w_all[pl.ds(pl.multiple_of((1 - k) * half, 128), half), :]
    for step in range(N_X):
        x = lax.rem(column + step, N_X)
        y_keep[step] = y_all[x * N_K + k]
        y_send[step] = y_all[x * N_K + 1 - k]


def product_and_grams(place, ancestor, gathered):
    f32, bf16 = jnp.float32, jnp.bfloat16
    half = 3 * WIDTH // 2
    wide = 2 * WIDTH
    return pl.pallas_call(
        product_kernel,
        in_specs=[SMEM] + [VMEM] * 18,
        out_specs=[VMEM] * 4,
        out_shape=[
            jax.ShapeDtypeStruct((half, WIDTH), f32),
            jax.ShapeDtypeStruct((half, WIDTH), f32),
            jax.ShapeDtypeStruct((N_X, ROWS, wide), f32),
            jax.ShapeDtypeStruct((N_X, ROWS, wide), f32),
        ],
        scratch_shapes=[
            pltpu.VMEM((1536, wide), bf16),
            pltpu.VMEM((1536, wide), bf16),
            pltpu.VMEM((384, wide), bf16),
            pltpu.VMEM((384, wide), bf16),
            pltpu.VMEM((3 * WIDTH, WIDTH), f32),
            pltpu.VMEM((N_COL, ROWS, wide), f32),
        ],
        compiler_params=pltpu.CompilerParams(vmem_limit_bytes=24 * 1024 * 1024),
        name="product_and_grams",
    )(place, ancestor, *gathered)


def at_owner(value, axis):
    count = lax.axis_size(axis)
    parts = value.reshape(count, value.shape[0] // count, *value.shape[1:])
    return lax.all_to_all(parts, axis, 0, 0, tiled=True)


def copies_of(value, axis):
    copies = jnp.broadcast_to(value[None], (lax.axis_size(axis), *value.shape))
    return lax.all_to_all(copies, axis, 0, 0, tiled=True)


def inverse_kernel(y0, y1, y2, y3, masks, above, out):
    rows = (y0[...] + y1[...]) + (y2[...] + y3[...])
    one = -rows[:, :WIDTH] * masks[:, :WIDTH]
    out[:, :WIDTH] = one
    out[:, WIDTH:] = -(rows[:, WIDTH:] + dot(one, above[...])) * masks[:, WIDTH:]


def inverse_rows(parts, masks, panel_above):
    return pl.pallas_call(
        inverse_kernel,
        in_specs=[VMEM] * 6,
        out_specs=VMEM,
        out_shape=jax.ShapeDtypeStruct((ROWS, 2 * WIDTH), jnp.float32),
        compiler_params=SMALL,
        name="inverse_rows",
    )(*parts, masks, panel_above)


def pick_kernel(place, owner, rows, one, keep, send):
    column, k = place[1], place[2]
    one[...] = rows[:, :WIDTH]
    keep[...] = jnp.zeros(keep.shape, jnp.float32)
    send[...] = jnp.zeros(send.shape, jnp.float32)
    for tile in range(TILES):
        mine = owner[tile]
        rank = jnp.int32(0)
        for earlier in range(tile):
            rank = rank + jnp.where(owner[earlier] == mine, 1, 0)
        rank = jnp.minimum(rank, CAP - 1)
        step = lax.rem(lax.div(mine, N_K) + N_X - column, N_X)
        core = lax.rem(mine, N_K)
        values = rows[tile * TILE_ROWS : (tile + 1) * TILE_ROWS, WIDTH:]

        @pl.when(core == k)
        def _():
            keep[step * CAP + rank] = values

        @pl.when(core != k)
        def _():
            send[step * CAP + rank] = values


def pick_tiles(place, tile_owner, rows):
    tiles = jax.ShapeDtypeStruct((N_X * CAP, TILE_ROWS, WIDTH), jnp.float32)
    return pl.pallas_call(
        pick_kernel,
        in_specs=[SMEM, SMEM, VMEM],
        out_specs=[VMEM] * 3,
        out_shape=[jax.ShapeDtypeStruct((ROWS, WIDTH), jnp.float32), tiles, tiles],
        compiler_params=SMALL,
        name="pick_tiles",
    )(place, tile_owner.reshape(-1), rows)


def slots_kernel(place, p0, p1, p2, p3, out):
    column, k = place[1], place[2]
    for step, part in enumerate((p0, p1, p2, p3)):
        x = lax.rem(column + N_X - step, N_X)
        for source, core in ((0, k), (1, 1 - k)):
            for slot in range(CAP):
                out[(x * N_K + core) * CAP + slot] = part[source, slot]


def fill_slots(place, parts):
    return pl.pallas_call(
        slots_kernel,
        in_specs=[SMEM] + [VMEM] * 4,
        out_specs=VMEM,
        out_shape=jax.ShapeDtypeStruct((N_COL * CAP, TILE_ROWS, WIDTH), jnp.float32),
        compiler_params=SMALL,
        name="fill_slots",
    )(place, *parts)


def sent_over_x(keep, arrived):
    shape = (N_X, CAP, TILE_ROWS, WIDTH)
    pairs = jnp.stack([keep.reshape(shape), arrived.reshape(shape)], axis=1)
    parts = [pairs[0]]
    for step in range(1, N_X):
        parts.append(lax.ppermute(pairs[step], ROW_COL, along_x(step)))
    return parts


def final_kernel(place, half, other, square_one, square_two, above, diag_one, cross_two, diag_two, w):
    rows = half.shape[0]
    first = pl.multiple_of(place[2] * rows, 128)
    second = pl.multiple_of((1 - place[2]) * rows, 128)
    w[pl.ds(first, rows), :] = half[...]
    w[pl.ds(second, rows), :] = other[...]
    w_cross = w[WIDTH : 2 * WIDTH]
    rows_dims = ((0,), (0,))
    one = square_one[...] + w[:WIDTH]
    over = split(above[...])
    cross = w_cross - three_pass(split(one), over, ((1,), (0,)))
    diag_one[...] = one
    cross_two[...] = cross
    twice = three_pass(split(w_cross), over, rows_dims) + three_pass(over, split(cross), rows_dims)
    diag_two[...] = square_two[...] + w[2 * WIDTH :] - twice


def final_blocks(place, half, other, square_one, square_two, panel_above):
    block = jax.ShapeDtypeStruct((WIDTH, WIDTH), jnp.float32)
    return pl.pallas_call(
        final_kernel,
        in_specs=[SMEM] + [VMEM] * 5,
        out_specs=[VMEM] * 3,
        out_shape=[block] * 3,
        scratch_shapes=[pltpu.VMEM((3 * WIDTH, WIDTH), jnp.float32)],
        compiler_params=SMALL,
        name="final_blocks",
    )(place, half, other, square_one, square_two, panel_above)


def local(
    ancestor_inverse,
    panel_one,
    struct_one,
    lower_one,
    panel_two,
    struct_two,
    panel_above,
    lower_two,
    tile_owner,
):
    start = (lax.axis_index(ROW) * N_COL + lax.axis_index(COL)) * ROWS
    place = jnp.stack([lax.axis_index(name) for name in ("row_0", "col_0", "col_1", "row_1")])
    place = place.astype(jnp.int32)
    panels, masks = masked_panels(
        start.astype(jnp.int32)[None], struct_one, struct_two, panel_one, panel_two
    )
    block = lax.ppermute(panels, ROW_COL, to_column(0))
    far_block = lax.ppermute(panels, ROW_COL, to_column(2))
    sibling = lax.ppermute(panels, ROW_COL, other_core())
    block, far_block, sibling = lax.optimization_barrier((block, far_block, sibling))
    pair = jnp.stack([panels, sibling])
    both = jnp.concatenate([block, far_block], axis=0)
    ring = [both]
    up = down = both
    for _ in range(3):
        up = lax.ppermute(up, ROW_COL, along_z(1))
        down = lax.ppermute(down, ROW_COL, along_z(-1))
        ring += [up, down]
    last_own = lax.ppermute(up[:ROWS], ROW_COL, along_z(1))
    last_far = lax.ppermute(down[ROWS:], ROW_COL, along_z(-1))
    batches = (
        jnp.concatenate([part[:ROWS] for part in ring[:5]], axis=0),
        jnp.concatenate([part[:ROWS] for part in ring[5:]] + [last_own], axis=0),
    )
    above = [lax.ppermute(batch, ROW_COL, along_y(-1)) for batch in batches]
    below = [lax.ppermute(batch, ROW_COL, along_y(1)) for batch in batches]
    row_panels = [pair]
    for step in range(1, N_X):
        row_panels.append(lax.ppermute(pair, ROW_COL, along_x(step)))
    w_keep, w_send, y_keep, y_send = product_and_grams(
        place,
        ancestor_inverse,
        (*ring, last_own, last_far, *above, *below, *row_panels),
    )
    w_own = w_keep + lax.ppermute(w_send, ROW_COL, other_core())
    y_send, w_own = lax.optimization_barrier((y_send, w_own))
    y_own = y_keep + lax.ppermute(y_send, ROW_COL, other_core())
    y_parts = [y_own[0]]
    for step in range(1, N_X):
        y_parts.append(lax.ppermute(y_own[step], ROW_COL, along_x(step)))
    w_part = jnp.sum(at_owner(w_own, PLANE), axis=0)
    inverses = inverse_rows(y_parts, masks, panel_above)
    w_part, inverses = lax.optimization_barrier((w_part, inverses))
    inverses = lax.ppermute(inverses, ROW_COL, moves(result_place))
    w_parts, inverses = lax.optimization_barrier((copies_of(w_part, "row_1"), inverses))
    w_half = copies_of(jnp.sum(w_parts, axis=0), PLANE).reshape(w_own.shape)
    inverse_one, keep, send = pick_tiles(place, tile_owner, inverses)
    arrived = lax.ppermute(send, ROW_COL, other_core())
    w_half, arrived = lax.optimization_barrier((w_half, arrived))
    w_other = lax.ppermute(w_half, ROW_COL, other_core())
    parts = sent_over_x(keep, arrived)
    square_one = dot(lower_one, lower_one, ((0,), (0,)))
    square_two = dot(lower_two, lower_two, ((0,), (0,)))
    diag_one, cross_two, diag_two = final_blocks(
        place, w_half, w_other, square_one, square_two, panel_above
    )
    parts, diag_two = lax.optimization_barrier((parts, diag_two))
    delivered = fill_slots(place, parts)
    return (inverse_one, diag_one, cross_two, diag_two, delivered)


def solution(mesh):
    finer = Mesh(mesh.devices.reshape(4, 8, 4, 2), ("row_0", "row_1", "col_0", "col_1"))
    return jax.shard_map(
        local,
        mesh=finer,
        in_specs=(
            P(ROW, COL),
            P(ROW_COL, None),
            P(),
            P(),
            P(ROW_COL, None),
            P(),
            P(),
            P(),
            P(COL_ROW, None),
        ),
        out_specs=(P(COL_ROW, None), P(), P(), P(), P(ROW_COL, None, None)),
        check_vma=False,
    )
```

```python
import jax
import jax.numpy as jnp
from jax import lax
from jax.experimental import pallas as pl
from jax.experimental.pallas import tpu as pltpu
from jax.sharding import Mesh
from jax.sharding import PartitionSpec as P

CAP = 2
COL = ("col_0", "col_1")
ROW = ("row_0", "row_1")
ROW_COL = ROW + COL
COL_ROW = COL + ROW
PLANE = ("row_0", "col_0")
N_Y, N_Z, N_X, N_K = 4, 8, 4, 2
N_ROW, N_COL = N_Y * N_Z, N_X * N_K
ROWS = 48
WIDTH = 256
TILES, TILE_ROWS = 6, 8
WAIT = 100_000_000
SMALL = pltpu.CompilerParams(vmem_limit_bytes=6 * 1024 * 1024)
SMEM = pl.BlockSpec(memory_space=pltpu.SMEM)
VMEM = pl.BlockSpec(memory_space=pltpu.VMEM)


def device(y, z, x, k):
    return ((y * N_Z + z) * N_X + x) * N_K + k


def moves(place):
    return [
        (device(y, z, x, k), device(*place(y, z, x, k)))
        for y in range(N_Y)
        for z in range(N_Z)
        for x in range(N_X)
        for k in range(N_K)
    ]


def to_column(step):
    return moves(lambda y, z, x, k: ((x + step) % N_Y, 7 - z if k else z, y, z // 4))


def result_place(y, z, x, k):
    column, row = divmod((y * N_Z + z) * N_COL + x * N_K + k, N_ROW)
    return (row // N_Z, row % N_Z, column // N_K, column % N_K)


def along_y(step):
    return moves(lambda y, z, x, k: ((y + step) % N_Y, z, x, k))


def along_z(step):
    return moves(lambda y, z, x, k: (y, (z + step) % N_Z, x, k))


def along_x(step):
    return moves(lambda y, z, x, k: (y, z, (x + step) % N_X, k))


def other_core():
    return moves(lambda y, z, x, k: (y, z, x, 1 - k))


def mask_kernel(
    start, one_hbm, two_hbm, panel_one_hbm, panel_two_hbm, panels, masks,
    one_ref, two_ref, panel_one, panel_two, sems,
):
    pairs = (
        (one_hbm, one_ref),
        (two_hbm, two_ref),
        (panel_one_hbm, panel_one),
        (panel_two_hbm, panel_two),
    )
    copies = [
        pltpu.make_async_copy(source, target, sems.at[i])
        for i, (source, target) in enumerate(pairs)
    ]
    for copy in copies:
        copy.start()
    for copy in copies:
        copy.wait()
    rows = start[0] + lax.broadcasted_iota(jnp.int32, (ROWS, 128), 0)
    for part, (listed, panel) in enumerate(((one_ref, panel_one), (two_ref, panel_two))):
        hit = jnp.zeros((ROWS, 128), jnp.float32)
        for line in range(listed.shape[0]):
            hit = jnp.where(listed[line : line + 1, :] == rows, 1.0, hit)
        mask = jnp.broadcast_to(jnp.max(hit, axis=1, keepdims=True), (ROWS, WIDTH))
        columns = slice(part * WIDTH, (part + 1) * WIDTH)
        masks[:, columns] = mask
        panels[:, columns] = panel[...] * mask


def masked_panels(start, struct_one, struct_two, panel_one, panel_two):
    shape = jax.ShapeDtypeStruct((ROWS, 2 * WIDTH), jnp.float32)
    one, two = struct_one.reshape(-1, 128), struct_two.reshape(-1, 128)
    fetched = [
        pltpu.with_memory_space_constraint(value, pltpu.HBM)
        for value in (one, two, panel_one, panel_two)
    ]
    return pl.pallas_call(
        mask_kernel,
        in_specs=[SMEM] + [pl.BlockSpec(memory_space=pltpu.HBM)] * 4,
        out_specs=[VMEM] * 2,
        out_shape=[shape, shape],
        scratch_shapes=[
            pltpu.VMEM(one.shape, jnp.int32),
            pltpu.VMEM(two.shape, jnp.int32),
            pltpu.VMEM((ROWS, WIDTH), jnp.float32),
            pltpu.VMEM((ROWS, WIDTH), jnp.float32),
            pltpu.SemaphoreType.DMA((4,)),
        ],
        compiler_params=SMALL,
        name="masked_panels",
    )(start, *fetched)


def dot(left, right, dims=((1,), (0,)), precision=lax.Precision.HIGHEST):
    return lax.dot_general(
        left, right, (dims, ((), ())), precision=precision, preferred_element_type=jnp.float32
    )


def split(value):
    high = value.astype(jnp.bfloat16)
    return high, (value - high.astype(jnp.float32)).astype(jnp.bfloat16)


def three_pass(left, right, dims):
    (a, b), (c, d) = left, right

    def one(p, q):
        return lax.dot_general(p, q, (dims, ((), ())), preferred_element_type=jnp.float32)

    return one(a, c) + (one(a, d) + one(b, c))


RING = (0, -1, 1, -2, 2, -3, 3)
BATCHES = ((0, -1, 1, -2, 2), (-3, 3, 4))


def put_block(place, step, offset, values, high_ref, low_ref):
    y, k, z = place[0], place[2], place[3]
    x = lax.rem(y + step, N_X)
    at = lax.rem(z + N_Z + offset, N_Z)
    near = lax.div(at, 4) == k
    line = lax.rem(jnp.where(near, at, N_Z - 1 - at), 4)
    first = pl.multiple_of(line * 384 + x * 96 + jnp.where(near, 0, ROWS), 16)
    high, low = split(values)
    high_ref[pl.ds(first, ROWS), :] = high
    low_ref[pl.ds(first, ROWS), :] = low


def operands_kernel(place, a_ref, *refs):
    ring, last_own, above, below, rows = refs[:7], refs[7], refs[8], refs[9], refs[10:12]
    ah, al, xh, xl, rh, rl = refs[12:]
    column, k = place[1], place[2]
    ah[...], al[...] = split(a_ref[...])
    for offset, ref in zip(RING, ring):
        put_block(place, 0, offset, ref[:ROWS], xh, xl)
        put_block(place, 2, offset, ref[ROWS:], xh, xl)
    put_block(place, 0, 4, last_own[...], xh, xl)
    for step, ref in ((1, above), (3, below)):
        for i, offset in enumerate(BATCHES[0]):
            put_block(place, step, offset, ref[i * ROWS : (i + 1) * ROWS], xh, xl)
    for step in range(N_X):
        x = lax.rem(column + N_X - step, N_X)
        for r_ref, core in zip(rows, (k, 1 - k)):
            high, low = split(r_ref[step])
            at = pl.multiple_of((x * N_K + core) * ROWS, 16)
            rh[pl.ds(at, ROWS), :] = high
            rl[pl.ds(at, ROWS), :] = low


def operands(place, ancestor, arrays):
    shapes = [ancestor.shape] * 2 + [(1536, 2 * WIDTH)] * 2 + [(384, 2 * WIDTH)] * 2
    return pl.pallas_call(
        operands_kernel,
        in_specs=[SMEM] + [VMEM] * 13,
        out_specs=[VMEM] * 6,
        out_shape=[jax.ShapeDtypeStruct(shape, jnp.bfloat16) for shape in shapes],
        compiler_params=pltpu.CompilerParams(vmem_limit_bytes=16 * 1024 * 1024),
        name="operands",
    )(place, ancestor, *arrays)


def product_kernel(
    place, ah, al, rh, rl, last_far, above, below, xh_in, xl_in,
    w_keep, w_send, y_keep, y_send, xh, xl, w_all, y_all,
):
    column, k = place[1], place[2]
    put_block(place, 2, 4, last_far[...], xh, xl)
    for step, ref in ((1, above), (3, below)):
        for i, offset in enumerate(BATCHES[1]):
            put_block(place, step, offset, ref[i * ROWS : (i + 1) * ROWS], xh, xl)
    product = three_pass((ah[...], al[...]), (xh[...], xl[...]), ((1,), (0,)))
    for block in range(N_COL):
        y_all[block] = product[block * ROWS : (block + 1) * ROWS]
    high, low = split(product)
    rows_dims = ((0,), (0,))
    one = (rh[:, :WIDTH], rl[:, :WIDTH])
    two = (rh[:, WIDTH:], rl[:, WIDTH:])
    from_one = three_pass(one, (high, low), rows_dims)
    w_all[0:WIDTH, :] = from_one[:, :WIDTH]
    w_all[WIDTH : 2 * WIDTH, :] = from_one[:, WIDTH:]
    w_all[2 * WIDTH :, :] = three_pass(two, (high[:, WIDTH:], low[:, WIDTH:]), rows_dims)
    half = 3 * WIDTH // 2
    w_keep[...] = w_all[pl.ds(pl.multiple_of(k * half, 128), half), :]
    w_send[...] = w_all[pl.ds(pl.multiple_of((1 - k) * half, 128), half), :]
    for step in range(N_X):
        x = lax.rem(column + step, N_X)
        y_keep[step] = y_all[x * N_K + k]
        y_send[step] = y_all[x * N_K + 1 - k]


def product_and_grams(place, prepared, arrays):
    f32 = jnp.float32
    half = 3 * WIDTH // 2
    wide = 2 * WIDTH
    ah, al, xh, xl, rh, rl = prepared
    blocks = jax.ShapeDtypeStruct(xh.shape, xh.dtype)
    return pl.pallas_call(
        product_kernel,
        in_specs=[SMEM] + [VMEM] * 9,
        out_specs=[VMEM] * 6,
        out_shape=[
            jax.ShapeDtypeStruct((half, WIDTH), f32),
            jax.ShapeDtypeStruct((half, WIDTH), f32),
            jax.ShapeDtypeStruct((N_X, ROWS, wide), f32),
            jax.ShapeDtypeStruct((N_X, ROWS, wide), f32),
            blocks,
            blocks,
        ],
        input_output_aliases={8: 4, 9: 5},
        scratch_shapes=[
            pltpu.VMEM((3 * WIDTH, WIDTH), f32),
            pltpu.VMEM((N_COL, ROWS, wide), f32),
        ],
        compiler_params=pltpu.CompilerParams(vmem_limit_bytes=24 * 1024 * 1024),
        name="product_and_grams",
    )(place, ah, al, rh, rl, *arrays, xh, xl)[:4]


def at_owner(value, axis):
    count = lax.axis_size(axis)
    parts = value.reshape(count, value.shape[0] // count, *value.shape[1:])
    return lax.all_to_all(parts, axis, 0, 0, tiled=True)


def copies_of(value, axis):
    copies = jnp.broadcast_to(value[None], (lax.axis_size(axis), *value.shape))
    return lax.all_to_all(copies, axis, 0, 0, tiled=True)


def inverse_kernel(y0, y1, y2, y3, masks, above, out):
    rows = (y0[...] + y1[...]) + (y2[...] + y3[...])
    one = -rows[:, :WIDTH] * masks[:, :WIDTH]
    out[:, :WIDTH] = one
    out[:, WIDTH:] = -(rows[:, WIDTH:] + dot(one, above[...])) * masks[:, WIDTH:]


def inverse_rows(parts, masks, panel_above):
    return pl.pallas_call(
        inverse_kernel,
        in_specs=[VMEM] * 6,
        out_specs=VMEM,
        out_shape=jax.ShapeDtypeStruct((ROWS, 2 * WIDTH), jnp.float32),
        compiler_params=SMALL,
        name="inverse_rows",
    )(*parts, masks, panel_above)


def square_kernel(lower_one, lower_two, square_one, square_two):
    for lower, square in ((lower_one, square_one), (lower_two, square_two)):
        square[...] = dot(lower[...], lower[...], ((0,), (0,)))


def square_blocks(lower_one, lower_two):
    block = jax.ShapeDtypeStruct((WIDTH, WIDTH), jnp.float32)
    return pl.pallas_call(
        square_kernel,
        in_specs=[VMEM] * 2,
        out_specs=[VMEM] * 2,
        out_shape=[block] * 2,
        compiler_params=SMALL,
        cost_estimate=pl.CostEstimate(flops=0, transcendentals=0, bytes_accessed=WAIT),
        name="square_blocks",
    )(lower_one, lower_two)


def pick_kernel(place, owner, rows, one, keep, send):
    column, k = place[1], place[2]
    one[...] = rows[:, :WIDTH]
    keep[...] = jnp.zeros(keep.shape, jnp.float32)
    send[...] = jnp.zeros(send.shape, jnp.float32)
    for tile in range(TILES):
        mine = owner[tile]
        rank = jnp.int32(0)
        for earlier in range(tile):
            rank = rank + jnp.where(owner[earlier] == mine, 1, 0)
        rank = jnp.minimum(rank, CAP - 1)
        step = lax.rem(lax.div(mine, N_K) + N_X - column, N_X)
        core = lax.rem(mine, N_K)
        values = rows[tile * TILE_ROWS : (tile + 1) * TILE_ROWS, WIDTH:]

        @pl.when(core == k)
        def _():
            keep[step * CAP + rank] = values

        @pl.when(core != k)
        def _():
            send[step * CAP + rank] = values


def pick_tiles(place, tile_owner, rows):
    tiles = jax.ShapeDtypeStruct((N_X * CAP, TILE_ROWS, WIDTH), jnp.float32)
    return pl.pallas_call(
        pick_kernel,
        in_specs=[SMEM, SMEM, VMEM],
        out_specs=[VMEM] * 3,
        out_shape=[jax.ShapeDtypeStruct((ROWS, WIDTH), jnp.float32), tiles, tiles],
        compiler_params=SMALL,
        name="pick_tiles",
    )(place, tile_owner.reshape(-1), rows)


def slots_kernel(place, p0, p1, p2, p3, out):
    column, k = place[1], place[2]
    for step, part in enumerate((p0, p1, p2, p3)):
        x = lax.rem(column + N_X - step, N_X)
        for source, core in ((0, k), (1, 1 - k)):
            for slot in range(CAP):
                out[(x * N_K + core) * CAP + slot] = part[source, slot]


def fill_slots(place, parts):
    return pl.pallas_call(
        slots_kernel,
        in_specs=[SMEM] + [VMEM] * 4,
        out_specs=VMEM,
        out_shape=jax.ShapeDtypeStruct((N_COL * CAP, TILE_ROWS, WIDTH), jnp.float32),
        compiler_params=SMALL,
        name="fill_slots",
    )(place, *parts)


def sent_over_x(keep, arrived):
    shape = (N_X, CAP, TILE_ROWS, WIDTH)
    pairs = jnp.stack([keep.reshape(shape), arrived.reshape(shape)], axis=1)
    parts = [pairs[0]]
    for step in range(1, N_X):
        parts.append(lax.ppermute(pairs[step], ROW_COL, along_x(step)))
    return parts


def final_kernel(place, half, other, square_one, square_two, above, diag_one, cross_two, diag_two, w):
    rows = half.shape[0]
    first = pl.multiple_of(place[2] * rows, 128)
    second = pl.multiple_of((1 - place[2]) * rows, 128)
    w[pl.ds(first, rows), :] = half[...]
    w[pl.ds(second, rows), :] = other[...]
    w_cross = w[WIDTH : 2 * WIDTH]
    rows_dims = ((0,), (0,))
    one = square_one[...] + w[:WIDTH]
    over = split(above[...])
    cross = w_cross - three_pass(split(one), over, ((1,), (0,)))
    diag_one[...] = one
    cross_two[...] = cross
    twice = three_pass(split(w_cross), over, rows_dims) + three_pass(over, split(cross), rows_dims)
    diag_two[...] = square_two[...] + w[2 * WIDTH :] - twice


def final_blocks(place, half, other, square_one, square_two, panel_above):
    block = jax.ShapeDtypeStruct((WIDTH, WIDTH), jnp.float32)
    return pl.pallas_call(
        final_kernel,
        in_specs=[SMEM] + [VMEM] * 5,
        out_specs=[VMEM] * 3,
        out_shape=[block] * 3,
        scratch_shapes=[pltpu.VMEM((3 * WIDTH, WIDTH), jnp.float32)],
        compiler_params=SMALL,
        name="final_blocks",
    )(place, half, other, square_one, square_two, panel_above)


def local(
    ancestor_inverse,
    panel_one,
    struct_one,
    lower_one,
    panel_two,
    struct_two,
    panel_above,
    lower_two,
    tile_owner,
):
    start = (lax.axis_index(ROW) * N_COL + lax.axis_index(COL)) * ROWS
    place = jnp.stack([lax.axis_index(name) for name in ("row_0", "col_0", "col_1", "row_1")])
    place = place.astype(jnp.int32)
    panels, masks = masked_panels(
        start.astype(jnp.int32)[None], struct_one, struct_two, panel_one, panel_two
    )
    block = lax.ppermute(panels, ROW_COL, to_column(0))
    far_block = lax.ppermute(panels, ROW_COL, to_column(2))
    over_x = [panels]
    for step in range(1, N_X):
        over_x.append(lax.ppermute(panels, ROW_COL, along_x(step)))
    block, far_block, over_x = lax.optimization_barrier((block, far_block, over_x))
    both = jnp.concatenate([block, far_block], axis=0)
    ring = [both]
    up = down = both
    for _ in range(3):
        up = lax.ppermute(up, ROW_COL, along_z(1))
        down = lax.ppermute(down, ROW_COL, along_z(-1))
        ring += [up, down]
    last_own = lax.ppermute(up[:ROWS], ROW_COL, along_z(1))
    last_far = lax.ppermute(down[ROWS:], ROW_COL, along_z(-1))
    batches = (
        jnp.concatenate([part[:ROWS] for part in ring[:5]], axis=0),
        jnp.concatenate([part[:ROWS] for part in ring[5:]] + [last_own], axis=0),
    )
    above = [lax.ppermute(batch, ROW_COL, along_y(-1)) for batch in batches]
    below = [lax.ppermute(batch, ROW_COL, along_y(1)) for batch in batches]
    own_core = jnp.stack(over_x)
    row_panels = (own_core, lax.ppermute(own_core, ROW_COL, other_core()))
    prepared = operands(
        place, ancestor_inverse, (*ring, last_own, above[0], below[0], *row_panels)
    )
    w_keep, w_send, y_keep, y_send = product_and_grams(
        place, prepared, (last_far, above[1], below[1])
    )
    w_own = w_keep + lax.ppermute(w_send, ROW_COL, other_core())
    y_send, w_own = lax.optimization_barrier((y_send, w_own))
    y_own = y_keep + lax.ppermute(y_send, ROW_COL, other_core())
    y_parts = [y_own[0]]
    for step in range(1, N_X):
        y_parts.append(lax.ppermute(y_own[step], ROW_COL, along_x(step)))
    w_part = jnp.sum(at_owner(w_own, PLANE), axis=0)
    inverses = inverse_rows(y_parts, masks, panel_above)
    w_part, inverses, lower_one, lower_two = lax.optimization_barrier(
        (w_part, inverses, lower_one, lower_two)
    )
    squares = square_blocks(lower_one, lower_two)
    inverses = lax.ppermute(inverses, ROW_COL, moves(result_place))
    w_parts, inverses, squares = lax.optimization_barrier(
        (copies_of(w_part, "row_1"), inverses, squares)
    )
    square_one, square_two = squares
    w_half = copies_of(jnp.sum(w_parts, axis=0), PLANE).reshape(w_own.shape)
    inverse_one, keep, send = pick_tiles(place, tile_owner, inverses)
    arrived = lax.ppermute(send, ROW_COL, other_core())
    parts = sent_over_x(keep, arrived)
    w_half, _ = lax.optimization_barrier((w_half, parts))
    w_other = lax.ppermute(w_half, ROW_COL, other_core())
    diag_one, cross_two, diag_two = final_blocks(
        place, w_half, w_other, square_one, square_two, panel_above
    )
    delivered = fill_slots(place, parts)
    return (inverse_one, diag_one, cross_two, diag_two, delivered)


def solution(mesh):
    finer = Mesh(mesh.devices.reshape(4, 8, 4, 2), ("row_0", "row_1", "col_0", "col_1"))
    return jax.shard_map(
        local,
        mesh=finer,
        in_specs=(
            P(ROW, COL),
            P(ROW_COL, None),
            P(),
            P(),
            P(ROW_COL, None),
            P(),
            P(),
            P(),
            P(COL_ROW, None),
        ),
        out_specs=(P(COL_ROW, None), P(), P(), P(), P(ROW_COL, None, None)),
        check_vma=False,
    )
```

```python
import jax
import jax.numpy as jnp
from jax import lax
from jax.experimental import pallas as pl
from jax.experimental.pallas import tpu as pltpu
from jax.sharding import Mesh
from jax.sharding import PartitionSpec as P

CAP = 2
COL = ("col_0", "col_1")
ROW = ("row_0", "row_1")
ROW_COL = ROW + COL
COL_ROW = COL + ROW
PLANE = ("row_0", "col_0")
N_Y, N_Z, N_X, N_K = 4, 8, 4, 2
N_ROW, N_COL = N_Y * N_Z, N_X * N_K
ROWS = 48
WIDTH = 256
TILES, TILE_ROWS = 6, 8
WAIT = 100_000_000
SMALL = pltpu.CompilerParams(vmem_limit_bytes=6 * 1024 * 1024)
SMEM = pl.BlockSpec(memory_space=pltpu.SMEM)
VMEM = pl.BlockSpec(memory_space=pltpu.VMEM)


def device(y, z, x, k):
    return ((y * N_Z + z) * N_X + x) * N_K + k


def moves(place):
    return [
        (device(y, z, x, k), device(*place(y, z, x, k)))
        for y in range(N_Y)
        for z in range(N_Z)
        for x in range(N_X)
        for k in range(N_K)
    ]


def to_column(step):
    return moves(lambda y, z, x, k: ((x + step) % N_Y, 7 - z if k else z, y, z // 4))


def result_place(y, z, x, k):
    column, row = divmod((y * N_Z + z) * N_COL + x * N_K + k, N_ROW)
    return (row // N_Z, row % N_Z, column // N_K, column % N_K)


def along_y(step):
    return moves(lambda y, z, x, k: ((y + step) % N_Y, z, x, k))


def along_z(step):
    return moves(lambda y, z, x, k: (y, (z + step) % N_Z, x, k))


def along_x(step):
    return moves(lambda y, z, x, k: (y, z, (x + step) % N_X, k))


def other_core():
    return moves(lambda y, z, x, k: (y, z, x, 1 - k))


def mask_kernel(
    start, one_hbm, two_hbm, panel_one_hbm, panel_two_hbm, panels, masks,
    one_ref, two_ref, panel_one, panel_two, sems,
):
    pairs = (
        (one_hbm, one_ref),
        (two_hbm, two_ref),
        (panel_one_hbm, panel_one),
        (panel_two_hbm, panel_two),
    )
    copies = [
        pltpu.make_async_copy(source, target, sems.at[i])
        for i, (source, target) in enumerate(pairs)
    ]
    for copy in copies:
        copy.start()
    for copy in copies:
        copy.wait()
    rows = start[0] + lax.broadcasted_iota(jnp.int32, (ROWS, 128), 0)
    for part, (listed, panel) in enumerate(((one_ref, panel_one), (two_ref, panel_two))):
        hit = jnp.zeros((ROWS, 128), jnp.float32)
        for line in range(listed.shape[0]):
            hit = jnp.where(listed[line : line + 1, :] == rows, 1.0, hit)
        mask = jnp.broadcast_to(jnp.max(hit, axis=1, keepdims=True), (ROWS, WIDTH))
        columns = slice(part * WIDTH, (part + 1) * WIDTH)
        masks[:, columns] = mask
        panels[:, columns] = panel[...] * mask


def masked_panels(start, struct_one, struct_two, panel_one, panel_two):
    shape = jax.ShapeDtypeStruct((ROWS, 2 * WIDTH), jnp.float32)
    one, two = struct_one.reshape(-1, 128), struct_two.reshape(-1, 128)
    fetched = [
        pltpu.with_memory_space_constraint(value, pltpu.HBM)
        for value in (one, two, panel_one, panel_two)
    ]
    return pl.pallas_call(
        mask_kernel,
        in_specs=[SMEM] + [pl.BlockSpec(memory_space=pltpu.HBM)] * 4,
        out_specs=[VMEM] * 2,
        out_shape=[shape, shape],
        scratch_shapes=[
            pltpu.VMEM(one.shape, jnp.int32),
            pltpu.VMEM(two.shape, jnp.int32),
            pltpu.VMEM((ROWS, WIDTH), jnp.float32),
            pltpu.VMEM((ROWS, WIDTH), jnp.float32),
            pltpu.SemaphoreType.DMA((4,)),
        ],
        compiler_params=SMALL,
        name="masked_panels",
    )(start, *fetched)


def dot(left, right, dims=((1,), (0,)), precision=lax.Precision.HIGHEST):
    return lax.dot_general(
        left, right, (dims, ((), ())), precision=precision, preferred_element_type=jnp.float32
    )


def split(value):
    high = value.astype(jnp.bfloat16)
    return high, (value - high.astype(jnp.float32)).astype(jnp.bfloat16)


def three_pass(left, right, dims):
    (a, b), (c, d) = left, right

    def one(p, q):
        return lax.dot_general(p, q, (dims, ((), ())), preferred_element_type=jnp.float32)

    return one(a, c) + (one(a, d) + one(b, c))


RING = (0, -1, 1, -2, 2, -3, 3)
BATCHES = ((0, -1, 1, -2, 2), (-3, 3, 4))


def put_block(place, step, offset, values, high_ref, low_ref):
    y, k, z = place[0], place[2], place[3]
    x = lax.rem(y + step, N_X)
    at = lax.rem(z + N_Z + offset, N_Z)
    near = lax.div(at, 4) == k
    line = lax.rem(jnp.where(near, at, N_Z - 1 - at), 4)
    first = pl.multiple_of(line * 384 + x * 96 + jnp.where(near, 0, ROWS), 16)
    high, low = split(values)
    high_ref[pl.ds(first, ROWS), :] = high
    low_ref[pl.ds(first, ROWS), :] = low


def operands_kernel(place, a_ref, *refs):
    ring, last_own, above, below, rows = refs[:7], refs[7], refs[8], refs[9], refs[10:12]
    ah, al, xh, xl, rh, rl = refs[12:]
    column, k = place[1], place[2]
    ah[...], al[...] = split(a_ref[...])
    for offset, ref in zip(RING, ring):
        put_block(place, 0, offset, ref[:ROWS], xh, xl)
        put_block(place, 2, offset, ref[ROWS:], xh, xl)
    put_block(place, 0, 4, last_own[...], xh, xl)
    for step, ref in ((1, above), (3, below)):
        for i, offset in enumerate(BATCHES[0]):
            put_block(place, step, offset, ref[i * ROWS : (i + 1) * ROWS], xh, xl)
    for step in range(N_X):
        x = lax.rem(column + N_X - step, N_X)
        for r_ref, core in zip(rows, (k, 1 - k)):
            high, low = split(r_ref[step])
            at = pl.multiple_of((x * N_K + core) * ROWS, 16)
            rh[pl.ds(at, ROWS), :] = high
            rl[pl.ds(at, ROWS), :] = low


def operands(place, ancestor, arrays):
    shapes = [ancestor.shape] * 2 + [(1536, 2 * WIDTH)] * 2 + [(384, 2 * WIDTH)] * 2
    return pl.pallas_call(
        operands_kernel,
        in_specs=[SMEM] + [VMEM] * 13,
        out_specs=[VMEM] * 6,
        out_shape=[jax.ShapeDtypeStruct(shape, jnp.bfloat16) for shape in shapes],
        compiler_params=pltpu.CompilerParams(vmem_limit_bytes=16 * 1024 * 1024),
        name="operands",
    )(place, ancestor, *arrays)


def product_kernel(
    place, ah, al, rh, rl, last_far, above, below, xh_in, xl_in,
    w_keep, w_send, y_keep, y_send, xh, xl, w_all, y_all,
):
    column, k = place[1], place[2]
    put_block(place, 2, 4, last_far[...], xh, xl)
    for step, ref in ((1, above), (3, below)):
        for i, offset in enumerate(BATCHES[1]):
            put_block(place, step, offset, ref[i * ROWS : (i + 1) * ROWS], xh, xl)
    product = three_pass((ah[...], al[...]), (xh[...], xl[...]), ((1,), (0,)))
    for block in range(N_COL):
        y_all[block] = product[block * ROWS : (block + 1) * ROWS]
    high, low = split(product)
    rows_dims = ((0,), (0,))
    one = (rh[:, :WIDTH], rl[:, :WIDTH])
    two = (rh[:, WIDTH:], rl[:, WIDTH:])
    from_one = three_pass(one, (high, low), rows_dims)
    w_all[0:WIDTH, :] = from_one[:, :WIDTH]
    w_all[WIDTH : 2 * WIDTH, :] = from_one[:, WIDTH:]
    w_all[2 * WIDTH :, :] = three_pass(two, (high[:, WIDTH:], low[:, WIDTH:]), rows_dims)
    half = 3 * WIDTH // 2
    w_keep[...] = w_all[pl.ds(pl.multiple_of(k * half, 128), half), :]
    w_send[...] = w_all[pl.ds(pl.multiple_of((1 - k) * half, 128), half), :]
    for step in range(N_X):
        x = lax.rem(column + step, N_X)
        y_keep[step] = y_all[x * N_K + k]
        y_send[step] = y_all[x * N_K + 1 - k]


def product_and_grams(place, prepared, arrays):
    f32 = jnp.float32
    half = 3 * WIDTH // 2
    wide = 2 * WIDTH
    ah, al, xh, xl, rh, rl = prepared
    blocks = jax.ShapeDtypeStruct(xh.shape, xh.dtype)
    return pl.pallas_call(
        product_kernel,
        in_specs=[SMEM] + [VMEM] * 9,
        out_specs=[VMEM] * 6,
        out_shape=[
            jax.ShapeDtypeStruct((half, WIDTH), f32),
            jax.ShapeDtypeStruct((half, WIDTH), f32),
            jax.ShapeDtypeStruct((N_X, ROWS, wide), f32),
            jax.ShapeDtypeStruct((N_X, ROWS, wide), f32),
            blocks,
            blocks,
        ],
        input_output_aliases={8: 4, 9: 5},
        scratch_shapes=[
            pltpu.VMEM((3 * WIDTH, WIDTH), f32),
            pltpu.VMEM((N_COL, ROWS, wide), f32),
        ],
        compiler_params=pltpu.CompilerParams(vmem_limit_bytes=24 * 1024 * 1024),
        name="product_and_grams",
    )(place, ah, al, rh, rl, *arrays, xh, xl)[:4]


def at_owner(value, axis):
    count = lax.axis_size(axis)
    parts = value.reshape(count, value.shape[0] // count, *value.shape[1:])
    return lax.all_to_all(parts, axis, 0, 0, tiled=True)


def copies_of(value, axis):
    copies = jnp.broadcast_to(value[None], (lax.axis_size(axis), *value.shape))
    return lax.all_to_all(copies, axis, 0, 0, tiled=True)


def inverse_kernel(y0, y1, y2, y3, masks, above, out):
    rows = (y0[...] + y1[...]) + (y2[...] + y3[...])
    one = -rows[:, :WIDTH] * masks[:, :WIDTH]
    out[:, :WIDTH] = one
    out[:, WIDTH:] = -(rows[:, WIDTH:] + dot(one, above[...])) * masks[:, WIDTH:]


def inverse_rows(parts, masks, panel_above):
    return pl.pallas_call(
        inverse_kernel,
        in_specs=[VMEM] * 6,
        out_specs=VMEM,
        out_shape=jax.ShapeDtypeStruct((ROWS, 2 * WIDTH), jnp.float32),
        compiler_params=SMALL,
        name="inverse_rows",
    )(*parts, masks, panel_above)


def square_kernel(lower_one, lower_two, square_one, square_two):
    for lower, square in ((lower_one, square_one), (lower_two, square_two)):
        square[...] = dot(lower[...], lower[...], ((0,), (0,)))


def square_blocks(lower_one, lower_two):
    block = jax.ShapeDtypeStruct((WIDTH, WIDTH), jnp.float32)
    return pl.pallas_call(
        square_kernel,
        in_specs=[VMEM] * 2,
        out_specs=[VMEM] * 2,
        out_shape=[block] * 2,
        compiler_params=SMALL,
        cost_estimate=pl.CostEstimate(flops=0, transcendentals=0, bytes_accessed=WAIT),
        name="square_blocks",
    )(lower_one, lower_two)


def pick_kernel(place, owner, rows, one, keep, send):
    column, k = place[1], place[2]
    one[...] = rows[:, :WIDTH]
    keep[...] = jnp.zeros(keep.shape, jnp.float32)
    send[...] = jnp.zeros(send.shape, jnp.float32)
    for tile in range(TILES):
        mine = owner[tile]
        rank = jnp.int32(0)
        for earlier in range(tile):
            rank = rank + jnp.where(owner[earlier] == mine, 1, 0)
        rank = jnp.minimum(rank, CAP - 1)
        step = lax.rem(lax.div(mine, N_K) + N_X - column, N_X)
        core = lax.rem(mine, N_K)
        values = rows[tile * TILE_ROWS : (tile + 1) * TILE_ROWS, WIDTH:]

        @pl.when(core == k)
        def _():
            keep[step * CAP + rank] = values

        @pl.when(core != k)
        def _():
            send[step * CAP + rank] = values


def pick_tiles(place, tile_owner, rows):
    tiles = jax.ShapeDtypeStruct((N_X * CAP, TILE_ROWS, WIDTH), jnp.float32)
    return pl.pallas_call(
        pick_kernel,
        in_specs=[SMEM, SMEM, VMEM],
        out_specs=[VMEM] * 3,
        out_shape=[jax.ShapeDtypeStruct((ROWS, WIDTH), jnp.float32), tiles, tiles],
        compiler_params=SMALL,
        name="pick_tiles",
    )(place, tile_owner.reshape(-1), rows)


def slots_kernel(place, p0, p1, p2, p3, out):
    column, k = place[1], place[2]
    for step, part in enumerate((p0, p1, p2, p3)):
        x = lax.rem(column + N_X - step, N_X)
        for source, core in ((0, k), (1, 1 - k)):
            for slot in range(CAP):
                out[(x * N_K + core) * CAP + slot] = part[source, slot]


def fill_slots(place, parts):
    return pl.pallas_call(
        slots_kernel,
        in_specs=[SMEM] + [VMEM] * 4,
        out_specs=VMEM,
        out_shape=jax.ShapeDtypeStruct((N_COL * CAP, TILE_ROWS, WIDTH), jnp.float32),
        compiler_params=SMALL,
        name="fill_slots",
    )(place, *parts)


def sent_over_x(keep, arrived):
    shape = (N_X, CAP, TILE_ROWS, WIDTH)
    pairs = jnp.stack([keep.reshape(shape), arrived.reshape(shape)], axis=1)
    parts = [pairs[0]]
    for step in range(1, N_X):
        parts.append(lax.ppermute(pairs[step], ROW_COL, along_x(step)))
    return parts


def final_kernel(place, half, other, square_one, square_two, above, diag_one, cross_two, diag_two, w):
    rows = half.shape[0]
    first = pl.multiple_of(place[2] * rows, 128)
    second = pl.multiple_of((1 - place[2]) * rows, 128)
    w[pl.ds(first, rows), :] = half[...]
    w[pl.ds(second, rows), :] = other[...]
    w_cross = w[WIDTH : 2 * WIDTH]
    rows_dims = ((0,), (0,))
    one = square_one[...] + w[:WIDTH]
    over = split(above[...])
    cross = w_cross - three_pass(split(one), over, ((1,), (0,)))
    diag_one[...] = one
    cross_two[...] = cross
    twice = three_pass(split(w_cross), over, rows_dims) + three_pass(over, split(cross), rows_dims)
    diag_two[...] = square_two[...] + w[2 * WIDTH :] - twice


def final_blocks(place, half, other, square_one, square_two, panel_above):
    block = jax.ShapeDtypeStruct((WIDTH, WIDTH), jnp.float32)
    return pl.pallas_call(
        final_kernel,
        in_specs=[SMEM] + [VMEM] * 5,
        out_specs=[VMEM] * 3,
        out_shape=[block] * 3,
        scratch_shapes=[pltpu.VMEM((3 * WIDTH, WIDTH), jnp.float32)],
        compiler_params=SMALL,
        name="final_blocks",
    )(place, half, other, square_one, square_two, panel_above)


def local(
    ancestor_inverse,
    panel_one,
    struct_one,
    lower_one,
    panel_two,
    struct_two,
    panel_above,
    lower_two,
    tile_owner,
):
    start = (lax.axis_index(ROW) * N_COL + lax.axis_index(COL)) * ROWS
    place = jnp.stack([lax.axis_index(name) for name in ("row_0", "col_0", "col_1", "row_1")])
    place = place.astype(jnp.int32)
    panels, masks = masked_panels(
        start.astype(jnp.int32)[None], struct_one, struct_two, panel_one, panel_two
    )
    over_x = [panels]
    for step in range(1, N_X):
        over_x.append(lax.ppermute(panels, ROW_COL, along_x(step)))
    far_block = lax.ppermute(panels, ROW_COL, to_column(2))
    block = lax.ppermute(panels, ROW_COL, to_column(0))
    block, far_block, over_x = lax.optimization_barrier((block, far_block, over_x))
    both = jnp.concatenate([block, far_block], axis=0)
    ring = [both]
    up = down = both
    for _ in range(3):
        up = lax.ppermute(up, ROW_COL, along_z(1))
        down = lax.ppermute(down, ROW_COL, along_z(-1))
        ring += [up, down]
    last_own = lax.ppermute(up[:ROWS], ROW_COL, along_z(1))
    last_far = lax.ppermute(down[ROWS:], ROW_COL, along_z(-1))
    batches = (
        jnp.concatenate([part[:ROWS] for part in ring[:5]], axis=0),
        jnp.concatenate([part[:ROWS] for part in ring[5:]] + [last_own], axis=0),
    )
    above = [lax.ppermute(batch, ROW_COL, along_y(-1)) for batch in batches]
    below = [lax.ppermute(batch, ROW_COL, along_y(1)) for batch in batches]
    own_core = jnp.stack(over_x)
    row_panels = (own_core, lax.ppermute(own_core, ROW_COL, other_core()))
    prepared = operands(
        place, ancestor_inverse, (*ring, last_own, above[0], below[0], *row_panels)
    )
    w_keep, w_send, y_keep, y_send = product_and_grams(
        place, prepared, (last_far, above[1], below[1])
    )
    w_own = w_keep + lax.ppermute(w_send, ROW_COL, other_core())
    y_send, w_own = lax.optimization_barrier((y_send, w_own))
    y_own = y_keep + lax.ppermute(y_send, ROW_COL, other_core())
    y_parts = [y_own[0]]
    for step in range(1, N_X):
        y_parts.append(lax.ppermute(y_own[step], ROW_COL, along_x(step)))
    w_part = jnp.sum(at_owner(w_own, PLANE), axis=0)
    inverses = inverse_rows(y_parts, masks, panel_above)
    w_part, inverses, lower_one, lower_two = lax.optimization_barrier(
        (w_part, inverses, lower_one, lower_two)
    )
    squares = square_blocks(lower_one, lower_two)
    inverses = lax.ppermute(inverses, ROW_COL, moves(result_place))
    w_parts, inverses, squares = lax.optimization_barrier(
        (copies_of(w_part, "row_1"), inverses, squares)
    )
    square_one, square_two = squares
    w_half = copies_of(jnp.sum(w_parts, axis=0), PLANE).reshape(w_own.shape)
    inverse_one, keep, send = pick_tiles(place, tile_owner, inverses)
    arrived = lax.ppermute(send, ROW_COL, other_core())
    parts = sent_over_x(keep, arrived)
    w_half, _ = lax.optimization_barrier((w_half, parts))
    w_other = lax.ppermute(w_half, ROW_COL, other_core())
    diag_one, cross_two, diag_two = final_blocks(
        place, w_half, w_other, square_one, square_two, panel_above
    )
    delivered = fill_slots(place, parts)
    return (inverse_one, diag_one, cross_two, diag_two, delivered)


def solution(mesh):
    finer = Mesh(mesh.devices.reshape(4, 8, 4, 2), ("row_0", "row_1", "col_0", "col_1"))
    return jax.shard_map(
        local,
        mesh=finer,
        in_specs=(
            P(ROW, COL),
            P(ROW_COL, None),
            P(),
            P(),
            P(ROW_COL, None),
            P(),
            P(),
            P(),
            P(COL_ROW, None),
        ),
        out_specs=(P(COL_ROW, None), P(), P(), P(), P(ROW_COL, None, None)),
        check_vma=False,
    )
```
